32 devices in a mesh: cohort: 8 (over z, y), stripe: 4 (over x, core).
Axes of the slice: x: 2, y: 2, z: 4, core: 2. Of those that a mesh axis runs over, the one named last changes fastest.
Arguments:
- cohort_scores: bfloat16 [8, 18432, 256], P('cohort', 'stripe'), may hold values from -6 to 6
- allele_match: int32 [8, 18432], P('cohort', 'stripe'), may hold values from 0 to 18431, as said below
- allele_flip: int32 [8, 18432], P('cohort', 'stripe'), may hold values 0 or 1
- precision: float32 [8, 18432], P('cohort', 'stripe'), may hold values from 0.3 to 900
- reference_panel: bfloat16 [512, 18432], P(None, 'stripe'), may hold values from -20 to 20
- gene_weights: bfloat16 [64, 49, 4608], P('stripe'), may hold values from -0.09375 to 0.09375
- window_start: int32 [64], P('stripe'), may hold values from 0 to 17856, as said below
- window_length: int32 [64], P('stripe'), may hold values from 576 to 4608
Outputs:
- association: float32 [64, 49, 256], P('stripe', None, 'cohort')
The draws below stay inside these ranges and needn't reach their ends.
Inputs may be any that keep to these rules, and one draw needn't show every extreme that they name: `allele_match`: within each cohort every variant is matched by exactly one row. The 4608 rows of one device match exactly 1152 variants of each stripe, stripe s being variants s * 4608 to (s + 1) * 4608 - 1. `window_start`: genes 16 * s to 16 * (s + 1) - 1 have their window start in stripe s; every window ends within the 18432 variants.
All inputs are finite; a program needn't handle non-finite values. No bound on the sum of `allele_flip` on one device may be relied on, other than what follows from the above.
Results may differ from the reference program's by a relative error of at most 0.004.
Values may be sent and summed in bfloat16 or wider, within the bound.
A program may use at most 128 MiB of HBM per device.

```python
import math
import jax
import jax.numpy as jnp
from jax import lax

ROWS = 4608
GENES_DEV = 16
TRAITS = 256
TISSUES = 49
N_REF = 512
L_MAX = 4608
COHORTS = 8
STRIPES = 4
VARIANTS = 18432
GENES = 64


def draw_allele_match(key, part):
    cohort_keys = jax.random.split(key, COHORTS)

    def one_cohort(cohort_key):
        first_key, second_key = jax.random.split(cohort_key)
        orders = jax.vmap(lambda stripe_key: jax.random.permutation(stripe_key, ROWS))(jax.random.split(first_key, STRIPES))
        global_index = orders.astype(jnp.int32) + (jnp.arange(STRIPES, dtype=jnp.int32) * ROWS)[:, None]
        by_source = global_index.reshape(STRIPES, STRIPES, ROWS // STRIPES).transpose(1, 0, 2).reshape(STRIPES, ROWS)
        shuffled = jax.vmap(lambda row_key, row_values: row_values[jax.random.permutation(row_key, ROWS)])(jax.random.split(second_key, STRIPES), by_source)
        return shuffled.reshape(VARIANTS)
    return jax.vmap(one_cohort)(cohort_keys).astype(jnp.int32)


def draw_precision(key, part):
    first_key, second_key = jax.random.split(key)
    position = jnp.arange(COHORTS, dtype=jnp.float32) / max(COHORTS - 1, 1)
    rising = jnp.exp(math.log(3.0) * position)[:, None]
    cohort_size = jnp.exp(jax.random.uniform(first_key, (COHORTS, 1), minval=0.0, maxval=math.log(100.0))) * rising
    quality = jax.random.uniform(second_key, (COHORTS, VARIANTS), minval=0.5, maxval=1.0)
    return (cohort_size * quality).astype(jnp.float32)


def draw_reference_panel(key, part):
    base_key, column_key = jax.random.split(key, 2)
    base = jnp.clip(jax.random.normal(base_key, (N_REF, VARIANTS), jnp.float32), -6.0, 6.0)
    column_scale = jnp.exp(jax.random.uniform(column_key, (1, VARIANTS), minval=math.log(0.2), maxval=math.log(0.7)))
    values = base * column_scale
    return values.astype(jnp.bfloat16)


def gene_windows(key):
    length_key, offset_key = jax.random.split(jax.random.fold_in(key, 17))
    stripe_ids = jnp.arange(STRIPES, dtype=jnp.int32)[:, None]
    gene_ids = jnp.arange(GENES_DEV, dtype=jnp.int32)[None, :]
    spans_len = jax.random.randint(length_key, (STRIPES, GENES_DEV), L_MAX // 8, L_MAX + 1, dtype=jnp.int32)
    leading = gene_ids == 0
    final = stripe_ids == STRIPES - 1
    closing = jnp.logical_and(final, gene_ids == GENES_DEV - 1)
    spans_len = jnp.where(leading, L_MAX, spans_len)
    spans_len = jnp.where(closing, L_MAX // 8, spans_len)
    ranges = jnp.where(final, ROWS - spans_len + 1, ROWS)
    offsets = jax.random.randint(offset_key, (STRIPES, GENES_DEV), 0, ranges, dtype=jnp.int32)
    begins = stripe_ids * ROWS + offsets
    crossing = stripe_ids * ROWS + ROWS - spans_len // 2
    begins = jnp.where(jnp.logical_and(leading, jnp.logical_not(final)), crossing, begins)
    begins = jnp.where(closing, VARIANTS - L_MAX // 8, begins)
    return (begins.reshape(GENES).astype(jnp.int32), spans_len.reshape(GENES).astype(jnp.int32))


def draw_window_start(key, part):
    return gene_windows(key)[0]


def draw_window_length(key, part):
    return gene_windows(key)[1]


def touch_ends(entries, rng, least, top_value):
    shape = entries.shape
    index_at = [jax.random.randint(jax.random.fold_in(rng, axis), (), 0, shape[axis]) for axis in range(len(shape))]
    entries = entries.at[tuple(index_at)].set(least)
    longest = shape.index(max(shape))
    index_at[longest] = (index_at[longest] + 1) % shape[longest]
    return entries.at[tuple(index_at)].set(top_value)


def strengthened(entries, key, source, target, parts, factor):
    owner, partner = [(jnp.arange(entries.shape[dim]) // (entries.shape[dim] // parts)).reshape([-1 if axis == dim else 1 for axis in range(entries.ndim)]) for dim in (source, target)]
    chosen = jax.random.permutation(key, parts)[partner]
    strong = (owner == chosen) | (owner == (partner + parts // 2) % parts)
    return jnp.where(strong, factor * entries, entries)


def steps_of(rng, shape, cuts, least, top_value):
    level = 1.0
    for dim, parts in cuts:
        steps = jax.random.uniform(jax.random.fold_in(jax.random.fold_in(rng, 6), dim), (parts,), jnp.float32, least / len(cuts), top_value / len(cuts))
        level = level * jnp.repeat(jnp.exp(steps), shape[dim] // parts).reshape((-1,) + (1,) * (len(shape) - 1 - dim))
    return level


def scatter_about(stream_key, dims, spread, limit, cuts=(), held_as=jnp.bfloat16):
    values = spread * jax.random.normal(stream_key, dims, jnp.float32)
    if cuts:
        values = values * steps_of(stream_key, dims, cuts, -0.22, 0.18)
    return jnp.clip(values, -limit, limit).astype(held_as)


def noise_with(own_key, dims, scale, bound, cuts, heavy, kind=jnp.bfloat16):
    values = scale * jax.random.normal(own_key, dims, jnp.float32)
    if cuts:
        values = values * steps_of(own_key, dims, cuts, -0.22, 0.18)
    return jnp.clip(strengthened(values, jax.random.fold_in(own_key, 3), *heavy), -bound, bound).astype(kind)


def setup_inputs(seed: int = 0) -> dict:
    splits = jax.random.split(jax.random.key(seed), 9)
    cohort_scores = noise_with(splits[0], (COHORTS, VARIANTS, TRAITS), 1.0, 6.0, ((0, 8), (1, 4)), (0, 2, 8, 2.0))
    allele_match = draw_allele_match(jax.random.fold_in(splits[8], 71), 0)
    allele_flip = touch_ends((jax.random.randint(splits[2], (COHORTS, VARIANTS), 0, 3) < 1).astype(jnp.int32), jax.random.fold_in(splits[2], 1), 0, 1)
    precision = draw_precision(jax.random.fold_in(splits[8], 71), 0)
    reference_panel = draw_reference_panel(jax.random.fold_in(splits[8], 71), 0)
    gene_weights = scatter_about(splits[5], (GENES, TISSUES, L_MAX), L_MAX ** -0.5, 0.09375, ((0, 4),))
    window_start = draw_window_start(jax.random.fold_in(splits[8], 71), 0)
    window_length = draw_window_length(jax.random.fold_in(splits[8], 71), 0)
    return {"cohort_scores": cohort_scores, "allele_match": allele_match, "allele_flip": allele_flip, "precision": precision, "reference_panel": reference_panel, "gene_weights": gene_weights, "window_start": window_start, "window_length": window_length}


EPSILON = 1e-06

def reference(cohort_scores, allele_match, allele_flip, precision, reference_panel, gene_weights, window_start, window_length):

    def add_cohort(running, inputs):
        rows_here, match_here, flip_here, weight_here = inputs
        signs = (1 - 2 * flip_here).astype(jnp.bfloat16)
        flipped = rows_here * signs[:, None]
        aligned = jnp.zeros((VARIANTS, TRAITS), jnp.bfloat16).at[match_here.astype(jnp.int32)].set(flipped)
        weighted = (jnp.sqrt(weight_here)[:, None] * aligned).astype(jnp.bfloat16)
        return (running + weighted.astype(jnp.float32), None)
    summed, _ = lax.scan(add_cohort, jnp.zeros((VARIANTS, TRAITS), jnp.float32), (cohort_scores, allele_match, allele_flip, precision))
    total_weight = lax.optimization_barrier(jnp.sum(precision, axis=0))
    combined = (summed.T / jnp.sqrt(total_weight)[None, :]).astype(jnp.bfloat16)
    panel_ext = jnp.concatenate([reference_panel, jnp.zeros((N_REF, L_MAX), jnp.bfloat16)], axis=1)
    score_ext = jnp.concatenate([combined, jnp.zeros((TRAITS, L_MAX), jnp.bfloat16)], axis=1)

    def one_gene(inputs):
        weight_gene, begin, size = inputs
        keep = jnp.arange(L_MAX) < size
        masked = jnp.where(keep[None, :], weight_gene, jnp.zeros_like(weight_gene))
        columns = lax.dynamic_slice(panel_ext, (jnp.int32(0), begin.astype(jnp.int32)), (N_REF, L_MAX))
        projected = jnp.dot(columns, masked.T, preferred_element_type=jnp.float32)
        variance = lax.optimization_barrier(jnp.sum(projected * projected, axis=0)) / N_REF
        window = lax.dynamic_slice(score_ext, (jnp.int32(0), begin.astype(jnp.int32)), (TRAITS, L_MAX))
        numerator = jnp.dot(masked, window.T, preferred_element_type=jnp.float32)
        return numerator / jnp.sqrt(variance + EPSILON)[:, None]
    return lax.map(one_gene, (gene_weights, window_start, window_length))
```

```python
import functools

import jax
import jax.numpy as jnp
from jax import lax
from jax.experimental import pallas as pl
from jax.experimental.pallas import tpu as pltpu
from jax.sharding import PartitionSpec as P

EPSILON = 1e-06


def passed_along(block, axis, distance):
    devices = range(lax.axis_size(axis))
    route = [(i - distance, i) for i in devices if i - distance in devices]
    return lax.ppermute(block, axis, route)


def running_count(member):
    rows, columns = member.shape
    block = 128 if rows % 128 == 0 else rows
    parts = member.astype(jnp.float32).reshape(rows // block, block, columns)
    inner = jnp.einsum(
        "ij,bjc->bic",
        jnp.tril(jnp.ones((block, block), jnp.float32)),
        parts,
        precision=lax.Precision.HIGHEST,
    )
    outer = jnp.einsum(
        "ab,bc->ac",
        jnp.tril(jnp.ones((rows // block, rows // block), jnp.float32), -1),
        inner[:, -1, :],
        precision=lax.Precision.HIGHEST,
    )
    return (inner + outer[:, None, :]).reshape(rows, columns).astype(jnp.int32)


def general_device(
    cohort_scores,
    allele_match,
    allele_flip,
    precision,
    reference_panel,
    gene_weights,
    window_start,
    window_length,
):
    row_count = cohort_scores.shape[1]
    trait_count = cohort_scores.shape[2]
    stripe_count = lax.axis_size("stripe")
    cohort_count = lax.axis_size("cohort")
    bucket_rows = row_count // stripe_count
    block_traits = trait_count // cohort_count
    person_count = reference_panel.shape[0]
    gene_count = gene_weights.shape[0]
    tissue_count = gene_weights.shape[1]
    window_span = gene_weights.shape[2]
    step_width = min(512, window_span)
    first_variant = lax.axis_index("stripe") * row_count
    target = allele_match[0] // row_count
    inside = allele_match[0] - target * row_count
    member = (target[:, None] == jnp.arange(stripe_count, dtype=jnp.int32)[None, :]).astype(
        jnp.int32
    )
    ranking = jnp.sum(running_count(member) * member, axis=1) - 1
    placing = target * bucket_rows + ranking
    signs = (1 - 2 * allele_flip[0]).astype(jnp.bfloat16)
    flipped = cohort_scores[0] * signs[:, None]
    outgoing = jnp.zeros((row_count, trait_count), jnp.bfloat16).at[placing].set(flipped)
    out_keys = jnp.zeros((row_count,), jnp.int32).at[placing].set(inside)
    got_rows, got_keys = (
        lax.all_to_all(
            outgoing.reshape(stripe_count, bucket_rows, trait_count),
            "stripe",
            split_axis=0,
            concat_axis=0,
            tiled=True,
        ),
        lax.all_to_all(
            out_keys.reshape(stripe_count, bucket_rows),
            "stripe",
            split_axis=0,
            concat_axis=0,
            tiled=True,
        ),
    )
    aligned = (
        jnp.zeros((row_count, trait_count), jnp.bfloat16)
        .at[got_keys.reshape(row_count)]
        .set(got_rows.reshape(row_count, trait_count))
    )
    own_weight = precision[0]
    weighted = (jnp.sqrt(own_weight)[:, None] * aligned).astype(jnp.bfloat16)
    total_weight = lax.psum(own_weight, "cohort")
    received = lax.all_to_all(weighted, "cohort", split_axis=1, concat_axis=1, tiled=True)
    summed = jnp.sum(
        received.reshape(row_count, cohort_count, block_traits).astype(jnp.float32), axis=1
    )
    combined = (summed.T / jnp.sqrt(total_weight)[None, :]).astype(jnp.bfloat16)
    joined = jnp.concatenate([reference_panel, combined], axis=0)
    moved = passed_along(joined, "stripe", -1)
    panel_rim = moved[:person_count]
    score_rim = moved[person_count:]
    panel_ext = jnp.concatenate([reference_panel, panel_rim], axis=1)
    score_ext = jnp.concatenate([combined, score_rim], axis=1)

    def weight_block(gene, block, size):
        offset = block * step_width
        piece = lax.dynamic_slice(
            gene_weights[gene], (jnp.int32(0), offset), (tissue_count, step_width)
        )
        keep = offset + jnp.arange(step_width, dtype=jnp.int32) < size
        return jnp.where(keep[None, :], piece, jnp.zeros_like(piece))

    def window_variance(gene, size):
        begin = window_start[gene] - first_variant

        def add_block(block, running):
            columns = lax.dynamic_slice(
                panel_ext, (jnp.int32(0), begin + block * step_width), (person_count, step_width)
            )
            piece = weight_block(gene, block, size)
            return running + lax.dot_general(
                columns, piece, (((1,), (1,)), ((), ())), preferred_element_type=jnp.float32
            )

        blocks_needed = (size + step_width - 1) // step_width
        projected = lax.fori_loop(
            0, blocks_needed, add_block, jnp.zeros((person_count, tissue_count), jnp.float32)
        )
        return jnp.sum(projected * projected, axis=0) / person_count

    def window_score(gene):
        begin = window_start[gene] - first_variant
        size = window_length[gene]

        def add_block(block, running):
            window = lax.dynamic_slice(
                score_ext, (jnp.int32(0), begin + block * step_width), (block_traits, step_width)
            )
            piece = weight_block(gene, block, size)
            return running + lax.dot_general(
                piece, window, (((1,), (1,)), ((), ())), preferred_element_type=jnp.float32
            )

        blocks_needed = (size + step_width - 1) // step_width
        return lax.fori_loop(
            0, blocks_needed, add_block, jnp.zeros((tissue_count, block_traits), jnp.float32)
        )

    empty = jnp.zeros((gene_count, tissue_count), jnp.float32)

    def every_gene(gene, partial_value):
        return partial_value.at[gene].set(window_variance(gene, window_length[gene]))

    variance = lax.fori_loop(0, gene_count, every_gene, empty)

    def score_gene(gene, partial_value):
        return partial_value.at[gene].set(window_score(gene))

    numerator = lax.fori_loop(
        0, gene_count, score_gene, jnp.zeros((gene_count, tissue_count, block_traits), jnp.float32)
    )
    return numerator / jnp.sqrt(variance + EPSILON)[:, :, None]

MESH = pl.DeviceIdType.MESH
BF16 = jnp.bfloat16
F32 = jnp.float32
I32 = jnp.int32
Y_COUNT = 2
STRIPES = 4
HALVES = 2
CHUNKS = 6
BIN_ROWS = 64
ABSENT = -1024.0
PIECES = 3


def spread_column(row):
    return jnp.transpose(jnp.broadcast_to(row, (128, 128)))


def iota(shape, dim):
    return lax.broadcasted_iota(I32, shape, dim)


def one_kernel(
    z_count,
    traits,
    persons,
    begin_ref,
    size_ref,
    match_ref,
    flip_ref,
    precision_ref,
    scores_hbm,
    panel_hbm,
    weights_hbm,
    out_ref,
    scores,
    panel,
    panel_rim,
    weights,
    hot_bin,
    bin_row,
    place_row,
    slot_row,
    sign_row,
    count_total,
    enc,
    base,
    got_enc,
    got_base,
    starts,
    packed,
    got_first,
    got_second,
    own,
    y_got,
    pair,
    z_got,
    mine,
    rim,
    precisions,
    root,
    panel_turned,
    score_turned,
    projected,
    square_row,
    squares,
    in_sem,
    rim_send,
    rim_recv,
    e_send,
    e_recv,
    b_send,
    b_recv,
    start_sem,
    x_send,
    x_recv,
    y_send,
    y_recv,
    z_send,
    z_recv,
    w_send,
    w_recv,
    s_send,
    s_recv,
    p_send,
    p_recv,
):
    cohort = lax.axis_index("cohort")
    stripe = lax.axis_index("stripe")
    cohorts = z_count * Y_COUNT
    z, y = cohort // Y_COUNT, lax.rem(cohort, Y_COUNT)
    x, core = stripe // 2, lax.rem(stripe, 2)
    rows = match_ref.shape[1]
    bucket = rows // STRIPES
    piece = bucket // PIECES
    bins = rows // 128
    width = rows // CHUNKS
    half = traits // HALVES
    part = half // cohorts
    share = panel.shape[0]
    genes = begin_ref.shape[0]
    lines = weights.shape[0]
    got = (got_first, got_second)

    def partner(e):
        return lax.rem(x + e // 2, 2) * 2 + lax.rem(core + e, 2)

    scores_in = pltpu.make_async_copy(scores_hbm, scores, in_sem.at[0])
    panel_in = pltpu.make_async_copy(
        panel_hbm.at[pl.ds(pl.multiple_of(cohort * share, share), share)], panel, in_sem.at[1]
    )
    weights_in = pltpu.make_async_copy(weights_hbm, weights, in_sem.at[2])
    scores_in.start()
    panel_in.start()
    weights_in.start()

    barrier = pltpu.get_barrier_semaphore()
    for d in range(1, cohorts):
        pl.semaphore_signal(
            barrier, inc=1, device_id=(lax.rem(cohort + d, cohorts), stripe), device_id_type=MESH
        )
    for e in range(1, STRIPES):
        pl.semaphore_signal(barrier, inc=1, device_id=(cohort, partner(e)), device_id_type=MESH)

    def panel_copy():
        return pltpu.make_async_remote_copy(
            src_ref=panel,
            dst_ref=panel_rim,
            send_sem=p_send,
            recv_sem=p_recv,
            device_id=(cohort, lax.rem(stripe + STRIPES - 1, STRIPES)),
            device_id_type=MESH,
        )

    def precision_copy(d):
        return pltpu.make_async_remote_copy(
            src_ref=precision_ref,
            dst_ref=precisions.at[d],
            send_sem=w_send.at[d],
            recv_sem=w_recv.at[d],
            device_id=(lax.rem(cohort + d, cohorts), stripe),
            device_id_type=MESH,
        )

    def square_copy(d):
        return pltpu.make_async_remote_copy(
            src_ref=square_row,
            dst_ref=squares.at[d],
            send_sem=s_send.at[d],
            recv_sem=s_recv.at[d],
            device_id=(lax.rem(cohort + d, cohorts), stripe),
            device_id_type=MESH,
        )

    def enc_copy(e):
        there = pl.ds(pl.multiple_of(partner(e) * BIN_ROWS, BIN_ROWS), BIN_ROWS)
        return pltpu.make_async_remote_copy(
            src_ref=enc.at[there],
            dst_ref=got_enc.at[e],
            send_sem=e_send.at[e],
            recv_sem=e_recv.at[e],
            device_id=(cohort, partner(e)),
            device_id_type=MESH,
        )

    def base_copy(e):
        there = pl.ds(pl.multiple_of(partner(e) * BIN_ROWS, BIN_ROWS), BIN_ROWS)
        return pltpu.make_async_remote_copy(
            src_ref=base.at[there],
            dst_ref=got_base.at[e],
            send_sem=b_send.at[e],
            recv_sem=b_recv.at[e],
            device_id=(cohort, partner(e)),
            device_id_type=MESH,
        )

    def x_copy(h, e, p):
        here = pl.ds(p * (piece // 128), piece // 128)
        return pltpu.make_async_remote_copy(
            src_ref=packed.at[h, e, here],
            dst_ref=got[h].at[e, here],
            send_sem=x_send.at[h, e, p],
            recv_sem=x_recv.at[h, e, p],
            device_id=(cohort, partner(e)),
            device_id_type=MESH,
        )

    def y_copy(h, k):
        return pltpu.make_async_remote_copy(
            src_ref=own.at[h, k, 1 - y],
            dst_ref=y_got.at[h, k],
            send_sem=y_send.at[h, k],
            recv_sem=y_recv.at[h, k],
            device_id=(z * Y_COUNT + 1 - y, stripe),
            device_id_type=MESH,
        )

    def z_copy(h, k, d):
        other = lax.rem(z + d, z_count)
        return pltpu.make_async_remote_copy(
            src_ref=pair.at[h, k, other],
            dst_ref=z_got.at[h, k, d],
            send_sem=z_send.at[h, k, d],
            recv_sem=z_recv.at[h, k, d],
            device_id=(other * Y_COUNT + y, stripe),
            device_id_type=MESH,
        )

    def rim_copy(h, k):
        return pltpu.make_async_remote_copy(
            src_ref=mine.at[h, k],
            dst_ref=rim.at[h, k],
            send_sem=rim_send.at[h, k],
            recv_sem=rim_recv.at[h, k],
            device_id=(cohort, lax.rem(stripe + STRIPES - 1, STRIPES)),
            device_id_type=MESH,
        )

    match = match_ref[...]
    owner = jnp.zeros_like(match)
    for s in range(1, STRIPES):
        owner = owner + jnp.where(match >= s * rows, 1, 0)
    inside = match - owner * rows
    bin_row[...] = owner * BIN_ROWS + lax.shift_right_logical(inside, 7)
    place_row[...] = jnp.bitwise_and(inside, 127)
    sign_row[...] = (1 - 2 * flip_ref[...]).astype(F32)
    root[...] = jnp.sqrt(precision_ref[...])
    bin_count = STRIPES * BIN_ROWS
    span = 512
    count_total[...] = jnp.zeros_like(count_total)
    base[...] = jnp.zeros_like(base)

    def count(c, carry):
        here = pl.ds(pl.multiple_of(c * span, span), span)
        hot = jnp.where(bin_row[:, here] == iota((bin_count, span), 0), 1.0, 0.0).astype(BF16)
        low = jnp.where(place_row[:, here] == iota((128, span), 0), 1.0, 0.0).astype(BF16)
        hot_bin[:, here] = hot
        below = jnp.where(bin_row[:, here] < iota((bin_count, span), 0), 1, 0)
        for b in range(span // 128):
            base[...] += below[:, b * 128 : (b + 1) * 128]
        count_total[...] += lax.dot_general(
            low, hot, (((1,), (1,)), ((), ())), preferred_element_type=F32
        )
        return carry

    lax.fori_loop(0, rows // span, count, 0)

    pl.semaphore_wait(barrier, cohorts + STRIPES - 2)
    panel_in.wait()

    @pl.when(stripe > 0)
    def _():
        panel_copy().start()

    present = count_total[...]
    present16 = present.astype(BF16)
    before = jnp.where(iota((128, 128), 1) < iota((128, 128), 0), 1.0, 0.0).astype(BF16)
    within = jnp.dot(before, present16, preferred_element_type=F32)
    sums = jnp.dot(jnp.ones((128, 128), BF16), present16, preferred_element_type=F32)
    earlier = jnp.where(
        iota((bin_count, bin_count), 0) < iota((bin_count, bin_count), 1), 1.0, 0.0
    ).astype(BF16)
    first = jnp.dot(sums.astype(BF16), earlier, preferred_element_type=F32)
    coded = jnp.where(present > 0.5, within, ABSENT)
    base[...] = (
        jnp.broadcast_to(jnp.sum(base[...], axis=1, keepdims=True), base.shape)
        - lax.shift_right_logical(iota(base.shape, 0), BIN_ROWS.bit_length() - 1) * bucket
    )
    for b in range(bin_count // 128):
        enc[b * 128 : (b + 1) * 128] = jnp.transpose(coded[:, b * 128 : (b + 1) * 128])
    for e in range(1, STRIPES):
        enc_copy(e).start()
        base_copy(e).start()
    for d in range(1, cohorts):
        precision_copy(d).start()
    mine_rows = pl.ds(pl.multiple_of(stripe * BIN_ROWS, BIN_ROWS), BIN_ROWS)
    got_enc[0] = enc[mine_rows, :]
    got_base[0] = base[mine_rows, :]
    high = jnp.floor(first[0:8] * (1.0 / 64.0))
    table = jnp.concatenate([within, high, first[0:8] - 64.0 * high], axis=0).astype(BF16)

    lane = iota((traits, traits), 1)
    source = (
        (lane % half // part % z_count * Y_COUNT + lane % half // (half // Y_COUNT))
        * (traits // cohorts)
        + lane // half * part
        + lane % part
    )
    order = jnp.where(iota((traits, traits), 0) == source, 1.0, 0.0).astype(BF16)
    scores_in.wait()

    def rank(c, carry):
        here = pl.ds(pl.multiple_of(c * span, span), span)
        found = jnp.dot(table, hot_bin[:, here], preferred_element_type=F32)
        chosen = jnp.where(place_row[:, here] == iota((128, span), 0), found[:128], 0.0)
        slot_row[:, here] = (
            jnp.sum(chosen, axis=0, keepdims=True) + 64.0 * found[128:129] + found[136:137]
        )
        scores[here, :] = jnp.dot(
            scores[here, :], order, preferred_element_type=F32
        ).astype(BF16)
        return carry

    lax.fori_loop(0, rows // span, rank, 0)

    def pack(c, carry):
        e, p = STRIPES - 1 - c // PIECES, lax.rem(c, PIECES)
        low = (partner(e) * bucket + p * piece).astype(F32)
        total = jnp.zeros((piece, traits), F32)
        for q in range(4):
            here = slice(q * bucket, (q + 1) * bucket)
            hot = jnp.where(
                slot_row[:, here] - low == iota((piece, bucket), 0).astype(F32),
                sign_row[:, here],
                0.0,
            ).astype(BF16)
            total = total + jnp.dot(hot, scores[here, :], preferred_element_type=F32)
        for b in range(piece // 128):
            for h in range(HALVES):
                packed[h, e, p * (piece // 128) + b] = jnp.transpose(
                    total[b * 128 : (b + 1) * 128, h * half : (h + 1) * half]
                ).astype(BF16)

        @pl.when(e > 0)
        def _():
            x_copy(0, e, p).start()

        @pl.when(e == 1)
        def _():
            x_copy(1, e, p).start()

        return carry

    lax.fori_loop(0, STRIPES * PIECES, pack, 0)
    for e in (3, 2):
        for p in range(PIECES):
            x_copy(1, e, p).start()

    def turn_panel(side, offset):
        def one(b, carry):
            block = side[:, pl.ds(pl.multiple_of(b * 128, 128), 128)].astype(F32)
            panel_turned[pl.ds(pl.multiple_of(offset + b * 128, 128), 128), :] = jnp.transpose(
                jnp.concatenate([block] * (128 // share), axis=0)
            )
            return carry

        lax.fori_loop(0, bins, one, 0)

    turn_panel(panel, 0)
    weights_in.wait()

    @pl.when(stripe < STRIPES - 1)
    def _():
        panel_copy().wait_recv()

    turn_panel(panel_rim, rows)
    projected[...] = jnp.zeros_like(projected)
    for e in range(1, STRIPES):
        enc_copy(e).wait_recv()
        base_copy(e).wait_recv()
    starts_in = pltpu.make_async_copy(got_base, starts, start_sem)
    starts_in.start()
    starts_in.wait()

    def align(h, k):
        for b in range(width // 128):
            at = k * (width // 128) + b
            hots, lefts = [], []
            for e in range(STRIPES):
                low = starts[e, at, 0]
                q = jnp.minimum(lax.shift_right_logical(low, 7), bucket // 128 - 2)
                want = got_enc[e, pl.ds(at, 1), :] + (low - q * 128).astype(F32)
                hots.append(
                    jnp.where(want == iota((256, 128), 0).astype(F32), 1.0, 0.0).astype(BF16)
                )
                for step in range(2):
                    lefts.append(got[h][e, q + step] if e else packed[h, e, q + step])
            total = jnp.dot(
                jnp.concatenate(lefts, axis=1),
                jnp.concatenate(hots, axis=0),
                preferred_element_type=F32,
            )
            scaled = (total * root[:, pl.ds(pl.multiple_of(at * 128, 128), 128)]).astype(BF16)
            for yy in range(Y_COUNT):
                own[h, k, yy, :, b * 128 : (b + 1) * 128] = scaled[
                    yy * (half // 2) : (yy + 1) * (half // 2)
                ]
        y_copy(h, k).start()

    def pair_up(h, k):
        y_copy(h, k).wait_recv()
        both = own[h, k, y].astype(F32) + y_got[h, k].astype(F32)
        for zi in range(z_count):
            pair[h, k, zi] = both[zi * part : (zi + 1) * part].astype(BF16)
        for d in range(1, z_count):
            z_copy(h, k, d).start()

    def windows(side, k, first_gene, lanes_each):
        tiles = []
        place = iota((width, 128), 0) + k * width
        group = iota((1, 128), 1) // lanes_each
        count = 128 // lanes_each
        for u in range(2):
            value = None
            limit = jnp.zeros((1, 128), I32)
            for j in range(count):
                gene = first_gene + u * count + j
                piece_ = side[pl.ds(begin_ref[gene] + k * width, width), :]
                value = piece_ if j == 0 else jnp.where(group == j, piece_, value)
                limit = jnp.where(group == j, size_ref[gene], limit)
            tiles.append(jnp.where(place < limit, value, 0.0).astype(BF16))
        return jnp.concatenate(tiles, axis=1)

    def left(k):
        return weights[:, pl.ds(pl.multiple_of(k * width, width), width)]

    each = 128 // share * 2

    def project(k):
        def one(n, carry):
            projected[n] += jnp.dot(
                left(k), windows(panel_turned, k, n * each, share), preferred_element_type=F32
            )
            return carry

        lax.fori_loop(0, genes // each, one, 0)

    def finish(h, k):
        summed = pair[h, k, z].astype(F32)
        for d in range(1, z_count):
            z_copy(h, k, d).wait_recv()
            summed = summed + z_got[h, k, d].astype(F32)
        here = pl.ds(pl.multiple_of(k * width, width), width)
        mine[h, k] = (summed / root[:, here]).astype(BF16)

        @pl.when(stripe > 0)
        def _():
            rim_copy(h, k).start()

    def turn_scores(side, k, offset):
        for b in range(width // 128):
            here = slice(b * 128, (b + 1) * 128)
            block = jnp.concatenate([side[h, k, :, here] for h in range(HALVES)], axis=0)
            copies = 128 // (HALVES * part)
            score_turned[
                pl.ds(pl.multiple_of(offset + k * width + b * 128, 128), 128), :
            ] = jnp.transpose(jnp.concatenate([block.astype(F32)] * copies, axis=0))

    for e in range(1, STRIPES):
        for p in range(PIECES):
            x_copy(0, e, p).wait_recv()

    def first_half(k, carry):
        @pl.when(k < CHUNKS)
        def _():
            align(0, k)
            project(k)

        @pl.when(k >= 1)
        def _():
            pair_up(0, k - 1)

        return carry

    lax.fori_loop(0, CHUNKS + 1, first_half, 0)

    line_gene = jnp.bitwise_and(iota((lines, 1), 0), genes - 1)
    square = jnp.zeros((lines, 128), F32)
    for n in range(genes // each):
        for u in range(2):
            value = projected[n, :, u * 128 : (u + 1) * 128]
            gene = n * each + u * (each // 2) + iota((1, 128), 1) // share
            square = square + jnp.where(line_gene == gene, value * value, 0.0)
    blocks = square_row.shape[0]
    square = jnp.concatenate([square, jnp.zeros((blocks * 128 - lines, 128), F32)], axis=0)
    for b in range(blocks):
        square_row[b : b + 1, :] = jnp.sum(
            jnp.transpose(square[b * 128 : (b + 1) * 128]), axis=0, keepdims=True
        )
    for d in range(1, cohorts):
        square_copy(d).start()

    for e in range(1, STRIPES):
        for p in range(PIECES):
            x_copy(1, e, p).wait_recv()

    def second_half(k, carry):
        @pl.when(k < CHUNKS)
        def _():
            align(1, k)

        @pl.when(k >= 1)
        def _():
            pair_up(1, k - 1)

        return carry

    lax.fori_loop(0, CHUNKS + 1, second_half, 0)

    precision_sum = precision_ref[...]
    for d in range(1, cohorts):
        precision_copy(d).wait_recv()
        precision_sum = precision_sum + precisions[d]
    root[...] = jnp.sqrt(precision_sum)

    def last(k, carry):
        finish(0, k)
        finish(1, k)
        turn_scores(mine, k, 0)
        return carry

    lax.fori_loop(0, CHUNKS, last, 0)

    square_sum = square_row[...]
    for d in range(1, cohorts):
        square_copy(d).wait_recv()
        square_sum = square_sum + squares[d]
    spread = 1.0 / jnp.sqrt(square_sum / persons + EPSILON)
    scale = jnp.concatenate([spread_column(spread[b : b + 1]) for b in range(blocks)], axis=0)

    def rim_in(k, carry):
        @pl.when(stripe < STRIPES - 1)
        def _():
            for h in range(HALVES):
                rim_copy(h, k).wait_recv()

        turn_scores(rim, k, rows)
        return carry

    lax.fori_loop(0, CHUNKS, rim_in, 0)

    wide = 128 // (HALVES * part) * 2
    projected[0] = jnp.zeros(projected.shape[1:], F32)
    projected[1] = jnp.zeros(projected.shape[1:], F32)

    def score(c, carry):
        n, k = lax.rem(c, 2), c // 2
        projected[n] += jnp.dot(
            left(k), windows(score_turned, k, n * wide, HALVES * part), preferred_element_type=F32
        )
        return carry

    lax.fori_loop(0, 2 * CHUNKS, score, 0)
    total = jnp.zeros((lines, 128), F32)
    for n in range(2):
        for u in range(2):
            gene = n * wide + u * (wide // 2) + iota((1, 128), 1) // (HALVES * part)
            total = total + jnp.where(
                line_gene == gene, projected[n, :, u * 128 : (u + 1) * 128], 0.0
            )
    total = total + pltpu.roll(total, 64, 1)
    total = total + pltpu.roll(total, 32, 1)
    out_ref[...] = (total * scale[:lines])[:, : HALVES * part]

    for h in range(HALVES):
        for k in range(CHUNKS):
            y_copy(h, k).wait_send()
            for d in range(1, z_count):
                z_copy(h, k, d).wait_send()

            @pl.when(stripe > 0)
            def _():
                rim_copy(h, k).wait_send()

        for e in range(1, STRIPES):
            for p in range(PIECES):
                x_copy(h, e, p).wait_send()
    for e in range(1, STRIPES):
        enc_copy(e).wait_send()
        base_copy(e).wait_send()
    for d in range(1, cohorts):
        precision_copy(d).wait_send()
        square_copy(d).wait_send()

    @pl.when(stripe > 0)
    def _():
        panel_copy().wait_send()


def fast_device(
    cohort_scores,
    allele_match,
    allele_flip,
    precision,
    reference_panel,
    gene_weights,
    window_start,
    window_length,
):
    rows, traits = cohort_scores.shape[1:]
    cohorts = lax.axis_size("cohort")
    z_count = cohorts // Y_COUNT
    bucket = rows // STRIPES
    persons = reference_panel.shape[0]
    share = persons // cohorts
    genes, tissues, span = gene_weights.shape
    lines = genes * tissues
    width = rows // CHUNKS
    half = traits // HALVES
    part = half // cohorts
    blocks = -(-lines // 1024) * 8
    begin = window_start - lax.axis_index("stripe") * rows
    vmem = pl.BlockSpec(memory_space=pltpu.VMEM)
    smem = pl.BlockSpec(memory_space=pltpu.SMEM)
    hbm = pl.BlockSpec(memory_space=pl.ANY)
    dma = pltpu.SemaphoreType.DMA
    table = pl.pallas_call(
        functools.partial(one_kernel, z_count, traits, persons),
        out_shape=jax.ShapeDtypeStruct((lines, HALVES * part), F32),
        in_specs=[smem, smem, vmem, vmem, vmem, hbm, hbm, hbm],
        out_specs=vmem,
        scratch_shapes=[
            pltpu.VMEM((rows, traits), BF16),
            pltpu.VMEM((share, rows), BF16),
            pltpu.VMEM((share, rows), BF16),
            pltpu.VMEM((lines, span), BF16),
            pltpu.VMEM((STRIPES * BIN_ROWS, rows), BF16),
            pltpu.VMEM((1, rows), I32),
            pltpu.VMEM((1, rows), I32),
            pltpu.VMEM((1, rows), F32),
            pltpu.VMEM((1, rows), F32),
            pltpu.VMEM((128, STRIPES * BIN_ROWS), F32),
            pltpu.VMEM((STRIPES * BIN_ROWS, 128), F32),
            pltpu.VMEM((STRIPES * BIN_ROWS, 128), I32),
            pltpu.VMEM((STRIPES, BIN_ROWS, 128), F32),
            pltpu.VMEM((STRIPES, BIN_ROWS, 128), I32),
            pltpu.SMEM((STRIPES, BIN_ROWS, 128), I32),
            pltpu.VMEM((HALVES, STRIPES, bucket // 128, half, 128), BF16),
            pltpu.VMEM((STRIPES, bucket // 128, half, 128), BF16),
            pltpu.VMEM((STRIPES, bucket // 128, half, 128), BF16),
            pltpu.VMEM((HALVES, CHUNKS, Y_COUNT, half // 2, width), BF16),
            pltpu.VMEM((HALVES, CHUNKS, half // 2, width), BF16),
            pltpu.VMEM((HALVES, CHUNKS, z_count, part, width), BF16),
            pltpu.VMEM((HALVES, CHUNKS, z_count, part, width), BF16),
            pltpu.VMEM((HALVES, CHUNKS, part, width), BF16),
            pltpu.VMEM((HALVES, CHUNKS, part, width), BF16),
            pltpu.VMEM((cohorts, 1, rows), F32),
            pltpu.VMEM((1, rows), F32),
            pltpu.VMEM((2 * rows, 128), F32),
            pltpu.VMEM((2 * rows, 128), F32),
            pltpu.VMEM((genes * share // 256, lines, 256), F32),
            pltpu.VMEM((blocks, 128), F32),
            pltpu.VMEM((cohorts, blocks, 128), F32),
            dma((3,)),
            dma((HALVES, CHUNKS)),
            dma((HALVES, CHUNKS)),
            dma((STRIPES,)),
            dma((STRIPES,)),
            dma((STRIPES,)),
            dma((STRIPES,)),
            dma,
            dma((HALVES, STRIPES, PIECES)),
            dma((HALVES, STRIPES, PIECES)),
            dma((HALVES, CHUNKS)),
            dma((HALVES, CHUNKS)),
            dma((HALVES, CHUNKS, z_count)),
            dma((HALVES, CHUNKS, z_count)),
            dma((cohorts,)),
            dma((cohorts,)),
            dma((cohorts,)),
            dma((cohorts,)),
            dma,
            dma,
        ],
        compiler_params=pltpu.CompilerParams(
            collective_id=0, has_side_effects=True, vmem_limit_bytes=58 * 2**20
        ),
    )(
        begin,
        window_length,
        allele_match,
        allele_flip,
        precision,
        cohort_scores[0],
        reference_panel,
        jnp.transpose(gene_weights, (1, 0, 2)).reshape(lines, span),
    )
    return jnp.transpose(table.reshape(tissues, genes, HALVES * part), (1, 0, 2))


def on_device(cohort_scores, *others):
    rows, traits = cohort_scores.shape[1:]
    stripes = lax.axis_size("stripe")
    cohorts = lax.axis_size("cohort")
    persons = others[3].shape[0]
    genes, tissues, span = others[4].shape
    fits = (
        stripes == STRIPES
        and cohorts == 8
        and traits == 256
        and genes == 16
        and persons == 64 * cohorts
        and rows % (128 * PIECES * STRIPES) == 0
        and rows % (128 * CHUNKS) == 0
        and rows % 512 == 0
        and rows // 128 <= BIN_ROWS
        and rows // STRIPES >= 256
        and span == rows
        and tissues * genes <= 1024
    )
    if fits:
        return fast_device(cohort_scores, *others)
    return general_device(cohort_scores, *others)


def solution(mesh):
    in_specs = (
        P("cohort", "stripe", None),
        P("cohort", "stripe"),
        P("cohort", "stripe"),
        P("cohort", "stripe"),
        P(None, "stripe"),
        P("stripe", None, None),
        P("stripe"),
        P("stripe"),
    )
    out_specs = P("stripe", None, "cohort")
    return jax.shard_map(
        on_device, mesh=mesh, in_specs=in_specs, out_specs=out_specs, check_vma=False
    )
```

```python
import functools

import jax
import jax.numpy as jnp
from jax import lax
from jax.experimental import pallas as pl
from jax.experimental.pallas import tpu as pltpu
from jax.sharding import PartitionSpec as P

EPSILON = 1e-06


def passed_along(block, axis, distance):
    devices = range(lax.axis_size(axis))
    route = [(i - distance, i) for i in devices if i - distance in devices]
    return lax.ppermute(block, axis, route)


def running_count(member):
    rows, columns = member.shape
    block = 128 if rows % 128 == 0 else rows
    parts = member.astype(jnp.float32).reshape(rows // block, block, columns)
    inner = jnp.einsum(
        "ij,bjc->bic",
        jnp.tril(jnp.ones((block, block), jnp.float32)),
        parts,
        precision=lax.Precision.HIGHEST,
    )
    outer = jnp.einsum(
        "ab,bc->ac",
        jnp.tril(jnp.ones((rows // block, rows // block), jnp.float32), -1),
        inner[:, -1, :],
        precision=lax.Precision.HIGHEST,
    )
    return (inner + outer[:, None, :]).reshape(rows, columns).astype(jnp.int32)


def general_device(
    cohort_scores,
    allele_match,
    allele_flip,
    precision,
    reference_panel,
    gene_weights,
    window_start,
    window_length,
):
    row_count = cohort_scores.shape[1]
    trait_count = cohort_scores.shape[2]
    stripe_count = lax.axis_size("stripe")
    cohort_count = lax.axis_size("cohort")
    bucket_rows = row_count // stripe_count
    block_traits = trait_count // cohort_count
    person_count = reference_panel.shape[0]
    gene_count = gene_weights.shape[0]
    tissue_count = gene_weights.shape[1]
    window_span = gene_weights.shape[2]
    step_width = min(512, window_span)
    first_variant = lax.axis_index("stripe") * row_count
    target = allele_match[0] // row_count
    inside = allele_match[0] - target * row_count
    member = (target[:, None] == jnp.arange(stripe_count, dtype=jnp.int32)[None, :]).astype(
        jnp.int32
    )
    ranking = jnp.sum(running_count(member) * member, axis=1) - 1
    placing = target * bucket_rows + ranking
    signs = (1 - 2 * allele_flip[0]).astype(jnp.bfloat16)
    flipped = cohort_scores[0] * signs[:, None]
    outgoing = jnp.zeros((row_count, trait_count), jnp.bfloat16).at[placing].set(flipped)
    out_keys = jnp.zeros((row_count,), jnp.int32).at[placing].set(inside)
    got_rows, got_keys = (
        lax.all_to_all(
            outgoing.reshape(stripe_count, bucket_rows, trait_count),
            "stripe",
            split_axis=0,
            concat_axis=0,
            tiled=True,
        ),
        lax.all_to_all(
            out_keys.reshape(stripe_count, bucket_rows),
            "stripe",
            split_axis=0,
            concat_axis=0,
            tiled=True,
        ),
    )
    aligned = (
        jnp.zeros((row_count, trait_count), jnp.bfloat16)
        .at[got_keys.reshape(row_count)]
        .set(got_rows.reshape(row_count, trait_count))
    )
    own_weight = precision[0]
    weighted = (jnp.sqrt(own_weight)[:, None] * aligned).astype(jnp.bfloat16)
    total_weight = lax.psum(own_weight, "cohort")
    received = lax.all_to_all(weighted, "cohort", split_axis=1, concat_axis=1, tiled=True)
    summed = jnp.sum(
        received.reshape(row_count, cohort_count, block_traits).astype(jnp.float32), axis=1
    )
    combined = (summed.T / jnp.sqrt(total_weight)[None, :]).astype(jnp.bfloat16)
    joined = jnp.concatenate([reference_panel, combined], axis=0)
    moved = passed_along(joined, "stripe", -1)
    panel_rim = moved[:person_count]
    score_rim = moved[person_count:]
    panel_ext = jnp.concatenate([reference_panel, panel_rim], axis=1)
    score_ext = jnp.concatenate([combined, score_rim], axis=1)

    def weight_block(gene, block, size):
        offset = block * step_width
        piece = lax.dynamic_slice(
            gene_weights[gene], (jnp.int32(0), offset), (tissue_count, step_width)
        )
        keep = offset + jnp.arange(step_width, dtype=jnp.int32) < size
        return jnp.where(keep[None, :], piece, jnp.zeros_like(piece))

    def window_variance(gene, size):
        begin = window_start[gene] - first_variant

        def add_block(block, running):
            columns = lax.dynamic_slice(
                panel_ext, (jnp.int32(0), begin + block * step_width), (person_count, step_width)
            )
            piece = weight_block(gene, block, size)
            return running + lax.dot_general(
                columns, piece, (((1,), (1,)), ((), ())), preferred_element_type=jnp.float32
            )

        blocks_needed = (size + step_width - 1) // step_width
        projected = lax.fori_loop(
            0, blocks_needed, add_block, jnp.zeros((person_count, tissue_count), jnp.float32)
        )
        return jnp.sum(projected * projected, axis=0) / person_count

    def window_score(gene):
        begin = window_start[gene] - first_variant
        size = window_length[gene]

        def add_block(block, running):
            window = lax.dynamic_slice(
                score_ext, (jnp.int32(0), begin + block * step_width), (block_traits, step_width)
            )
            piece = weight_block(gene, block, size)
            return running + lax.dot_general(
                piece, window, (((1,), (1,)), ((), ())), preferred_element_type=jnp.float32
            )

        blocks_needed = (size + step_width - 1) // step_width
        return lax.fori_loop(
            0, blocks_needed, add_block, jnp.zeros((tissue_count, block_traits), jnp.float32)
        )

    empty = jnp.zeros((gene_count, tissue_count), jnp.float32)

    def every_gene(gene, partial_value):
        return partial_value.at[gene].set(window_variance(gene, window_length[gene]))

    variance = lax.fori_loop(0, gene_count, every_gene, empty)

    def score_gene(gene, partial_value):
        return partial_value.at[gene].set(window_score(gene))

    numerator = lax.fori_loop(
        0, gene_count, score_gene, jnp.zeros((gene_count, tissue_count, block_traits), jnp.float32)
    )
    return numerator / jnp.sqrt(variance + EPSILON)[:, :, None]

MESH = pl.DeviceIdType.MESH
BF16 = jnp.bfloat16
F32 = jnp.float32
I32 = jnp.int32
Y_COUNT = 2
STRIPES = 4
HALVES = 2
CHUNKS = 6
BIN_ROWS = 64
ABSENT = -1024.0
PIECES = 3


def spread_column(row):
    return jnp.transpose(jnp.broadcast_to(row, (128, 128)))


def iota(shape, dim):
    return lax.broadcasted_iota(I32, shape, dim)


def one_kernel(
    z_count,
    traits,
    persons,
    window_ref,
    size_ref,
    match_ref,
    flip_ref,
    precision_ref,
    scores_hbm,
    panel_hbm,
    weights_hbm,
    out_ref,
    scores,
    panel,
    panel_rim,
    weights,
    hot_bin,
    bin_row,
    place_row,
    slot_row,
    sign_row,
    count_total,
    enc,
    base,
    base_row,
    got_enc,
    got_base,
    starts,
    packed,
    got_first,
    got_second,
    own,
    y_got,
    pair,
    z_got,
    mine,
    rim,
    precisions,
    root,
    panel_turned,
    score_turned,
    projected,
    square_row,
    squares,
    in_sem,
    rim_send,
    rim_recv,
    e_send,
    e_recv,
    b_send,
    b_recv,
    start_sem,
    x_send,
    x_recv,
    y_send,
    y_recv,
    z_send,
    z_recv,
    w_send,
    w_recv,
    s_send,
    s_recv,
    p_send,
    p_recv,
):
    cohort = lax.axis_index("cohort")
    stripe = lax.axis_index("stripe")
    cohorts = z_count * Y_COUNT
    z, y = cohort // Y_COUNT, lax.rem(cohort, Y_COUNT)
    x, core = stripe // 2, lax.rem(stripe, 2)
    rows = match_ref.shape[1]
    bucket = rows // STRIPES
    piece = bucket // PIECES
    bins = rows // 128
    width = rows // CHUNKS
    half = traits // HALVES
    part = half // cohorts
    share = panel.shape[0]
    genes = window_ref.shape[0]
    lines = weights.shape[0]
    got = (got_first, got_second)

    def partner(e):
        return lax.rem(x + e // 2, 2) * 2 + lax.rem(core + e, 2)

    scores_in = pltpu.make_async_copy(scores_hbm, scores, in_sem.at[0])
    panel_in = pltpu.make_async_copy(
        panel_hbm.at[pl.ds(pl.multiple_of(cohort * share, share), share)], panel, in_sem.at[1]
    )
    weights_in = pltpu.make_async_copy(weights_hbm, weights, in_sem.at[2])
    scores_in.start()
    panel_in.start()
    weights_in.start()

    barrier = pltpu.get_barrier_semaphore()
    for d in range(1, cohorts):
        pl.semaphore_signal(
            barrier, inc=1, device_id=(lax.rem(cohort + d, cohorts), stripe), device_id_type=MESH
        )
    for e in range(1, STRIPES):
        pl.semaphore_signal(barrier, inc=1, device_id=(cohort, partner(e)), device_id_type=MESH)

    def panel_copy():
        return pltpu.make_async_remote_copy(
            src_ref=panel,
            dst_ref=panel_rim,
            send_sem=p_send,
            recv_sem=p_recv,
            device_id=(cohort, lax.rem(stripe + STRIPES - 1, STRIPES)),
            device_id_type=MESH,
        )

    def precision_copy(d):
        return pltpu.make_async_remote_copy(
            src_ref=precision_ref,
            dst_ref=precisions.at[d],
            send_sem=w_send.at[d],
            recv_sem=w_recv.at[d],
            device_id=(lax.rem(cohort + d, cohorts), stripe),
            device_id_type=MESH,
        )

    def square_copy(d):
        return pltpu.make_async_remote_copy(
            src_ref=square_row,
            dst_ref=squares.at[d],
            send_sem=s_send.at[d],
            recv_sem=s_recv.at[d],
            device_id=(lax.rem(cohort + d, cohorts), stripe),
            device_id_type=MESH,
        )

    def enc_copy(e):
        there = pl.ds(pl.multiple_of(partner(e) * BIN_ROWS, BIN_ROWS), BIN_ROWS)
        return pltpu.make_async_remote_copy(
            src_ref=enc.at[there],
            dst_ref=got_enc.at[e],
            send_sem=e_send.at[e],
            recv_sem=e_recv.at[e],
            device_id=(cohort, partner(e)),
            device_id_type=MESH,
        )

    def base_copy(e):
        return pltpu.make_async_remote_copy(
            src_ref=base_row,
            dst_ref=got_base.at[e],
            send_sem=b_send.at[e],
            recv_sem=b_recv.at[e],
            device_id=(cohort, partner(e)),
            device_id_type=MESH,
        )

    def x_copy(h, e, p):
        here = pl.ds(p * (piece // 128), piece // 128)
        return pltpu.make_async_remote_copy(
            src_ref=packed.at[h, e, here],
            dst_ref=got[h].at[e, here],
            send_sem=x_send.at[h, e, p],
            recv_sem=x_recv.at[h, e, p],
            device_id=(cohort, partner(e)),
            device_id_type=MESH,
        )

    def y_copy(h, k):
        return pltpu.make_async_remote_copy(
            src_ref=own.at[h, k, 1 - y],
            dst_ref=y_got.at[h, k],
            send_sem=y_send.at[h, k],
            recv_sem=y_recv.at[h, k],
            device_id=(z * Y_COUNT + 1 - y, stripe),
            device_id_type=MESH,
        )

    def z_copy(h, k, d):
        other = lax.rem(z + d, z_count)
        return pltpu.make_async_remote_copy(
            src_ref=pair.at[h, k, other],
            dst_ref=z_got.at[h, k, d],
            send_sem=z_send.at[h, k, d],
            recv_sem=z_recv.at[h, k, d],
            device_id=(other * Y_COUNT + y, stripe),
            device_id_type=MESH,
        )

    def rim_copy(h, k):
        return pltpu.make_async_remote_copy(
            src_ref=mine.at[h, k],
            dst_ref=rim.at[h, k],
            send_sem=rim_send.at[h, k],
            recv_sem=rim_recv.at[h, k],
            device_id=(cohort, lax.rem(stripe + STRIPES - 1, STRIPES)),
            device_id_type=MESH,
        )

    match = match_ref[...]
    owner = jnp.zeros_like(match)
    for s in range(1, STRIPES):
        owner = owner + jnp.where(match >= s * rows, 1, 0)
    inside = match - owner * rows
    bin_row[...] = owner * BIN_ROWS + lax.shift_right_logical(inside, 7)
    place_row[...] = jnp.bitwise_and(inside, 127)
    sign_row[...] = (1 - 2 * flip_ref[...]).astype(F32)
    root[...] = jnp.sqrt(precision_ref[...])
    pl.semaphore_wait(barrier, cohorts + STRIPES - 2)
    panel_in.wait()

    @pl.when(stripe > 0)
    def _():
        panel_copy().start()

    for d in range(1, cohorts):
        precision_copy(d).start()
    bin_count = STRIPES * BIN_ROWS
    span = 512
    count_total[...] = jnp.zeros_like(count_total)
    base[...] = jnp.zeros_like(base)

    def count(c, carry):
        here = pl.ds(pl.multiple_of(c * span, span), span)
        hot = jnp.where(bin_row[:, here] == iota((bin_count, span), 0), 1.0, 0.0).astype(BF16)
        low = jnp.where(place_row[:, here] == iota((128, span), 0), 1.0, 0.0).astype(BF16)
        hot_bin[:, here] = hot
        below = jnp.where(bin_row[:, here] < iota((bin_count, span), 0), 1, 0)
        for b in range(span // 128):
            base[...] += below[:, b * 128 : (b + 1) * 128]
        count_total[...] += lax.dot_general(
            low, hot, (((1,), (1,)), ((), ())), preferred_element_type=F32
        )
        return carry

    lax.fori_loop(0, rows // span, count, 0)

    present = count_total[...]
    present16 = present.astype(BF16)
    before = jnp.where(iota((128, 128), 1) < iota((128, 128), 0), 1.0, 0.0).astype(BF16)
    within = jnp.dot(before, present16, preferred_element_type=F32)
    sums = jnp.dot(jnp.ones((128, 128), BF16), present16, preferred_element_type=F32)
    earlier = jnp.where(
        iota((bin_count, bin_count), 0) < iota((bin_count, bin_count), 1), 1.0, 0.0
    ).astype(BF16)
    first = jnp.dot(sums.astype(BF16), earlier, preferred_element_type=F32)
    coded = jnp.where(present > 0.5, within, ABSENT)
    for b in range(bin_count // 128):
        here = slice(b * 128, (b + 1) * 128)
        base_row[:, here] = jnp.sum(
            jnp.transpose(base[here, :]), axis=0, keepdims=True
        ) - bucket * lax.shift_right_logical(
            iota((1, 128), 1) + b * 128, BIN_ROWS.bit_length() - 1
        )
    for b in range(bin_count // 128):
        enc[b * 128 : (b + 1) * 128] = jnp.transpose(coded[:, b * 128 : (b + 1) * 128])
    for e in range(1, STRIPES):
        enc_copy(e).start()
        base_copy(e).start()
    mine_rows = pl.ds(pl.multiple_of(stripe * BIN_ROWS, BIN_ROWS), BIN_ROWS)
    got_enc[0] = enc[mine_rows, :]
    got_base[0] = base_row[...]
    high = jnp.floor(first[0:8] * (1.0 / 64.0))
    table = jnp.concatenate([within, high, first[0:8] - 64.0 * high], axis=0).astype(BF16)

    lane = iota((traits, traits), 1)
    source = (
        (lane % half // part % z_count * Y_COUNT + lane % half // (half // Y_COUNT))
        * (traits // cohorts)
        + lane // half * part
        + lane % part
    )
    order = jnp.where(iota((traits, traits), 0) == source, 1.0, 0.0).astype(BF16)
    scores_in.wait()

    def rank(c, carry):
        here = pl.ds(pl.multiple_of(c * span, span), span)
        found = jnp.dot(table, hot_bin[:, here], preferred_element_type=F32)
        chosen = jnp.where(place_row[:, here] == iota((128, span), 0), found[:128], 0.0)
        slot_row[:, here] = (
            jnp.sum(chosen, axis=0, keepdims=True) + 64.0 * found[128:129] + found[136:137]
        )
        scores[here, :] = jnp.dot(
            scores[here, :], order, preferred_element_type=F32
        ).astype(BF16)
        return carry

    lax.fori_loop(0, rows // span, rank, 0)

    def pack(c, carry):
        e, p = STRIPES - 1 - c // PIECES, lax.rem(c, PIECES)
        low = (partner(e) * bucket + p * piece).astype(F32)
        total = jnp.zeros((piece, traits), F32)
        for q in range(4):
            here = slice(q * bucket, (q + 1) * bucket)
            hot = jnp.where(
                slot_row[:, here] - low == iota((piece, bucket), 0).astype(F32),
                sign_row[:, here],
                0.0,
            ).astype(BF16)
            total = total + jnp.dot(hot, scores[here, :], preferred_element_type=F32)
        for b in range(piece // 128):
            for h in range(HALVES):
                packed[h, e, p * (piece // 128) + b] = jnp.transpose(
                    total[b * 128 : (b + 1) * 128, h * half : (h + 1) * half]
                ).astype(BF16)

        @pl.when(e > 0)
        def _():
            x_copy(0, e, p).start()

        @pl.when(e == 1)
        def _():
            x_copy(1, e, p).start()

        return carry

    lax.fori_loop(0, STRIPES * PIECES, pack, 0)
    for e in (3, 2):
        for p in range(PIECES):
            x_copy(1, e, p).start()

    def turn_panel(side, offset):
        def one(k, carry):
            for b in range(width // 128):
                here = pl.multiple_of(k * width + b * 128, 128)
                block = side[:, pl.ds(here, 128)].astype(F32)
                panel_turned[pl.ds(pl.multiple_of(offset + here, 128), 128), :] = jnp.transpose(
                    jnp.concatenate([block] * (128 // share), axis=0)
                )
            return carry

        lax.fori_loop(0, CHUNKS, one, 0)

    turn_panel(panel, 0)
    weights_in.wait()

    @pl.when(stripe < STRIPES - 1)
    def _():
        panel_copy().wait_recv()

    turn_panel(panel_rim, rows)
    projected[...] = jnp.zeros_like(projected)
    for e in range(1, STRIPES):
        enc_copy(e).wait_recv()
        base_copy(e).wait_recv()
    starts_in = pltpu.make_async_copy(got_base, starts, start_sem)
    starts_in.start()
    starts_in.wait()

    def align(h, k):
        for b in range(width // 128):
            at = k * (width // 128) + b
            hots, lefts = [], []
            for e in range(STRIPES):
                low = starts[e, 0, stripe * BIN_ROWS + at]
                q = jnp.minimum(lax.shift_right_logical(low, 7), bucket // 128 - 2)
                want = got_enc[e, pl.ds(at, 1), :] + (low - q * 128).astype(F32)
                hots.append(
                    jnp.where(want == iota((256, 128), 0).astype(F32), 1.0, 0.0).astype(BF16)
                )
                for step in range(2):
                    lefts.append(got[h][e, q + step] if e else packed[h, e, q + step])
            total = jnp.dot(
                jnp.concatenate(lefts, axis=1),
                jnp.concatenate(hots, axis=0),
                preferred_element_type=F32,
            )
            scaled = (total * root[:, pl.ds(pl.multiple_of(at * 128, 128), 128)]).astype(BF16)
            for yy in range(Y_COUNT):
                own[h, k, yy, :, b * 128 : (b + 1) * 128] = scaled[
                    yy * (half // 2) : (yy + 1) * (half // 2)
                ]
        y_copy(h, k).start()

    def pair_up(h, k):
        y_copy(h, k).wait_recv()
        both = own[h, k, y].astype(F32) + y_got[h, k].astype(F32)
        for zi in range(z_count):
            pair[h, k, zi] = both[zi * part : (zi + 1) * part].astype(BF16)
        for d in range(1, z_count):
            z_copy(h, k, d).start()

    def windows(side, k, first_gene, lanes_each):
        tiles = []
        place = iota((width, 128), 0) + k * width
        group = iota((1, 128), 1) // lanes_each
        count = 128 // lanes_each
        for u in range(2):
            value = None
            limit = jnp.zeros((1, 128), I32)
            for j in range(count):
                gene = first_gene + u * count + j
                piece_ = side[pl.ds(jnp.clip(window_ref[gene] - stripe * rows, 0, rows) + k * width, width), :]
                value = piece_ if j == 0 else jnp.where(group == j, piece_, value)
                limit = jnp.where(group == j, size_ref[gene], limit)
            tiles.append(jnp.where(place < limit, value, 0.0).astype(BF16))
        return jnp.concatenate(tiles, axis=1)

    def left(k):
        return weights[:, pl.ds(pl.multiple_of(k * width, width), width)]

    each = 128 // share * 2

    groups = genes // each

    def project(step):
        for c in range(groups // 2):
            n = lax.rem(step * (groups // 2) + c, groups)
            k = step // 2
            projected[n] += jnp.dot(
                left(k), windows(panel_turned, k, n * each, share), preferred_element_type=F32
            )

    def finish(h, k):
        summed = pair[h, k, z].astype(F32)
        for d in range(1, z_count):
            z_copy(h, k, d).wait_recv()
            summed = summed + z_got[h, k, d].astype(F32)
        here = pl.ds(pl.multiple_of(k * width, width), width)
        mine[h, k] = (summed / root[:, here]).astype(BF16)

        @pl.when(stripe > 0)
        def _():
            rim_copy(h, k).start()

    def turn_scores(side, k, offset):
        for b in range(width // 128):
            here = slice(b * 128, (b + 1) * 128)
            block = jnp.concatenate([side[h, k, :, here] for h in range(HALVES)], axis=0)
            copies = 128 // (HALVES * part)
            score_turned[
                pl.ds(pl.multiple_of(offset + k * width + b * 128, 128), 128), :
            ] = jnp.transpose(jnp.concatenate([block.astype(F32)] * copies, axis=0))

    for e in range(1, STRIPES):
        for p in range(PIECES):
            x_copy(0, e, p).wait_recv()

    def first_half(k, carry):
        @pl.when(k < CHUNKS)
        def _():
            align(0, k)
            project(k)

        @pl.when(k >= 1)
        def _():
            pair_up(0, k - 1)

        return carry

    lax.fori_loop(0, CHUNKS + 1, first_half, 0)

    for e in range(1, STRIPES):
        for p in range(PIECES):
            x_copy(1, e, p).wait_recv()

    def second_half(k, carry):
        @pl.when(k < CHUNKS)
        def _():
            align(1, k)
            project(k + CHUNKS)

        @pl.when(k >= 1)
        def _():
            pair_up(1, k - 1)

        return carry

    lax.fori_loop(0, CHUNKS + 1, second_half, 0)

    line_gene = jnp.bitwise_and(iota((lines, 1), 0), genes - 1)
    square = jnp.zeros((lines, 128), F32)
    for n in range(genes // each):
        for u in range(2):
            value = projected[n, :, u * 128 : (u + 1) * 128]
            gene = n * each + u * (each // 2) + iota((1, 128), 1) // share
            square = square + jnp.where(line_gene == gene, value * value, 0.0)
    blocks = square_row.shape[0]
    square = jnp.concatenate([square, jnp.zeros((blocks * 128 - lines, 128), F32)], axis=0)
    for b in range(blocks):
        square_row[b : b + 1, :] = jnp.sum(
            jnp.transpose(square[b * 128 : (b + 1) * 128]), axis=0, keepdims=True
        )
    for d in range(1, cohorts):
        square_copy(d).start()

    precision_sum = precision_ref[...]
    for d in range(1, cohorts):
        precision_copy(d).wait_recv()
        precision_sum = precision_sum + precisions[d]
    root[...] = jnp.sqrt(precision_sum)

    def last(k, carry):
        finish(0, k)
        finish(1, k)
        turn_scores(mine, k, 0)
        return carry

    lax.fori_loop(0, CHUNKS, last, 0)

    square_sum = square_row[...]
    for d in range(1, cohorts):
        square_copy(d).wait_recv()
        square_sum = square_sum + squares[d]
    spread = 1.0 / jnp.sqrt(square_sum / persons + EPSILON)
    scale = jnp.concatenate([spread_column(spread[b : b + 1]) for b in range(blocks)], axis=0)

    def rim_in(k, carry):
        @pl.when(stripe < STRIPES - 1)
        def _():
            for h in range(HALVES):
                rim_copy(h, k).wait_recv()

        turn_scores(rim, k, rows)
        return carry

    lax.fori_loop(0, CHUNKS, rim_in, 0)

    wide = 128 // (HALVES * part) * 2
    projected[0] = jnp.zeros(projected.shape[1:], F32)
    projected[1] = jnp.zeros(projected.shape[1:], F32)

    def score(c, carry):
        n, k = lax.rem(c, 2), c // 2
        projected[n] += jnp.dot(
            left(k), windows(score_turned, k, n * wide, HALVES * part), preferred_element_type=F32
        )
        return carry

    lax.fori_loop(0, 2 * CHUNKS, score, 0)
    total = jnp.zeros((lines, 128), F32)
    for n in range(2):
        for u in range(2):
            gene = n * wide + u * (wide // 2) + iota((1, 128), 1) // (HALVES * part)
            total = total + jnp.where(
                line_gene == gene, projected[n, :, u * 128 : (u + 1) * 128], 0.0
            )
    total = total + pltpu.roll(total, 64, 1)
    total = total + pltpu.roll(total, 32, 1)
    out_ref[...] = (total * scale[:lines])[:, : HALVES * part]

    for h in range(HALVES):
        for k in range(CHUNKS):
            y_copy(h, k).wait_send()
            for d in range(1, z_count):
                z_copy(h, k, d).wait_send()

            @pl.when(stripe > 0)
            def _():
                rim_copy(h, k).wait_send()

        for e in range(1, STRIPES):
            for p in range(PIECES):
                x_copy(h, e, p).wait_send()
    for e in range(1, STRIPES):
        enc_copy(e).wait_send()
        base_copy(e).wait_send()
    for d in range(1, cohorts):
        precision_copy(d).wait_send()
        square_copy(d).wait_send()

    @pl.when(stripe > 0)
    def _():
        panel_copy().wait_send()


def fast_device(
    cohort_scores,
    allele_match,
    allele_flip,
    precision,
    reference_panel,
    gene_weights,
    window_start,
    window_length,
):
    rows, traits = cohort_scores.shape[1:]
    cohorts = lax.axis_size("cohort")
    z_count = cohorts // Y_COUNT
    bucket = rows // STRIPES
    persons = reference_panel.shape[0]
    share = persons // cohorts
    genes, tissues, span = gene_weights.shape
    lines = genes * tissues
    width = rows // CHUNKS
    half = traits // HALVES
    part = half // cohorts
    blocks = -(-lines // 1024) * 8
    vmem = pl.BlockSpec(memory_space=pltpu.VMEM)
    smem = pl.BlockSpec(memory_space=pltpu.SMEM)
    hbm = pl.BlockSpec(memory_space=pl.ANY)
    dma = pltpu.SemaphoreType.DMA
    table = pl.pallas_call(
        functools.partial(one_kernel, z_count, traits, persons),
        out_shape=jax.ShapeDtypeStruct((lines, HALVES * part), F32),
        in_specs=[smem, smem, vmem, vmem, vmem, hbm, hbm, hbm],
        out_specs=vmem,
        scratch_shapes=[
            pltpu.VMEM((rows, traits), BF16),
            pltpu.VMEM((share, rows), BF16),
            pltpu.VMEM((share, rows), BF16),
            pltpu.VMEM((lines, span), BF16),
            pltpu.VMEM((STRIPES * BIN_ROWS, rows), BF16),
            pltpu.VMEM((1, rows), I32),
            pltpu.VMEM((1, rows), I32),
            pltpu.VMEM((1, rows), F32),
            pltpu.VMEM((1, rows), F32),
            pltpu.VMEM((128, STRIPES * BIN_ROWS), F32),
            pltpu.VMEM((STRIPES * BIN_ROWS, 128), F32),
            pltpu.VMEM((STRIPES * BIN_ROWS, 128), I32),
            pltpu.VMEM((1, STRIPES * BIN_ROWS), I32),
            pltpu.VMEM((STRIPES, BIN_ROWS, 128), F32),
            pltpu.VMEM((STRIPES, 1, STRIPES * BIN_ROWS), I32),
            pltpu.SMEM((STRIPES, 1, STRIPES * BIN_ROWS), I32),
            pltpu.VMEM((HALVES, STRIPES, bucket // 128, half, 128), BF16),
            pltpu.VMEM((STRIPES, bucket // 128, half, 128), BF16),
            pltpu.VMEM((STRIPES, bucket // 128, half, 128), BF16),
            pltpu.VMEM((HALVES, CHUNKS, Y_COUNT, half // 2, width), BF16),
            pltpu.VMEM((HALVES, CHUNKS, half // 2, width), BF16),
            pltpu.VMEM((HALVES, CHUNKS, z_count, part, width), BF16),
            pltpu.VMEM((HALVES, CHUNKS, z_count, part, width), BF16),
            pltpu.VMEM((HALVES, CHUNKS, part, width), BF16),
            pltpu.VMEM((HALVES, CHUNKS, part, width), BF16),
            pltpu.VMEM((cohorts, 1, rows), F32),
            pltpu.VMEM((1, rows), F32),
            pltpu.VMEM((2 * rows, 128), F32),
            pltpu.VMEM((2 * rows, 128), F32),
            pltpu.VMEM((genes * share // 256, lines, 256), F32),
            pltpu.VMEM((blocks, 128), F32),
            pltpu.VMEM((cohorts, blocks, 128), F32),
            dma((3,)),
            dma((HALVES, CHUNKS)),
            dma((HALVES, CHUNKS)),
            dma((STRIPES,)),
            dma((STRIPES,)),
            dma((STRIPES,)),
            dma((STRIPES,)),
            dma,
            dma((HALVES, STRIPES, PIECES)),
            dma((HALVES, STRIPES, PIECES)),
            dma((HALVES, CHUNKS)),
            dma((HALVES, CHUNKS)),
            dma((HALVES, CHUNKS, z_count)),
            dma((HALVES, CHUNKS, z_count)),
            dma((cohorts,)),
            dma((cohorts,)),
            dma((cohorts,)),
            dma((cohorts,)),
            dma,
            dma,
        ],
        compiler_params=pltpu.CompilerParams(
            collective_id=0, has_side_effects=True, vmem_limit_bytes=58 * 2**20
        ),
    )(
        window_start,
        window_length,
        allele_match,
        allele_flip,
        precision,
        cohort_scores[0],
        reference_panel,
        jnp.transpose(gene_weights, (1, 0, 2)).reshape(lines, span),
    )
    return jnp.transpose(table.reshape(tissues, genes, HALVES * part), (1, 0, 2))


def on_device(cohort_scores, *others):
    rows, traits = cohort_scores.shape[1:]
    stripes = lax.axis_size("stripe")
    cohorts = lax.axis_size("cohort")
    persons = others[3].shape[0]
    genes, tissues, span = others[4].shape
    fits = (
        stripes == STRIPES
        and cohorts == 8
        and traits == 256
        and genes == 16
        and persons == 64 * cohorts
        and rows % (128 * PIECES * STRIPES) == 0
        and rows % (128 * CHUNKS) == 0
        and rows % 512 == 0
        and rows // 128 <= BIN_ROWS
        and rows // STRIPES >= 256
        and span == rows
        and tissues * genes <= 1024
    )
    if fits:
        return fast_device(cohort_scores, *others)
    return general_device(cohort_scores, *others)


def solution(mesh):
    in_specs = (
        P("cohort", "stripe", None),
        P("cohort", "stripe"),
        P("cohort", "stripe"),
        P("cohort", "stripe"),
        P(None, "stripe"),
        P("stripe", None, None),
        P("stripe"),
        P("stripe"),
    )
    out_specs = P("stripe", None, "cohort")
    return jax.shard_map(
        on_device, mesh=mesh, in_specs=in_specs, out_specs=out_specs, check_vma=False
    )
```

```python
import functools

import jax
import jax.numpy as jnp
from jax import lax
from jax.experimental import pallas as pl
from jax.experimental.pallas import tpu as pltpu
from jax.sharding import PartitionSpec as P

EPSILON = 1e-06


def passed_along(block, axis, distance):
    devices = range(lax.axis_size(axis))
    route = [(i - distance, i) for i in devices if i - distance in devices]
    return lax.ppermute(block, axis, route)


def running_count(member):
    rows, columns = member.shape
    block = 128 if rows % 128 == 0 else rows
    parts = member.astype(jnp.float32).reshape(rows // block, block, columns)
    inner = jnp.einsum(
        "ij,bjc->bic",
        jnp.tril(jnp.ones((block, block), jnp.float32)),
        parts,
        precision=lax.Precision.HIGHEST,
    )
    outer = jnp.einsum(
        "ab,bc->ac",
        jnp.tril(jnp.ones((rows // block, rows // block), jnp.float32), -1),
        inner[:, -1, :],
        precision=lax.Precision.HIGHEST,
    )
    return (inner + outer[:, None, :]).reshape(rows, columns).astype(jnp.int32)


def general_device(
    cohort_scores,
    allele_match,
    allele_flip,
    precision,
    reference_panel,
    gene_weights,
    window_start,
    window_length,
):
    row_count = cohort_scores.shape[1]
    trait_count = cohort_scores.shape[2]
    stripe_count = lax.axis_size("stripe")
    cohort_count = lax.axis_size("cohort")
    bucket_rows = row_count // stripe_count
    block_traits = trait_count // cohort_count
    person_count = reference_panel.shape[0]
    gene_count = gene_weights.shape[0]
    tissue_count = gene_weights.shape[1]
    window_span = gene_weights.shape[2]
    step_width = min(512, window_span)
    first_variant = lax.axis_index("stripe") * row_count
    target = allele_match[0] // row_count
    inside = allele_match[0] - target * row_count
    member = (target[:, None] == jnp.arange(stripe_count, dtype=jnp.int32)[None, :]).astype(
        jnp.int32
    )
    ranking = jnp.sum(running_count(member) * member, axis=1) - 1
    placing = target * bucket_rows + ranking
    signs = (1 - 2 * allele_flip[0]).astype(jnp.bfloat16)
    flipped = cohort_scores[0] * signs[:, None]
    outgoing = jnp.zeros((row_count, trait_count), jnp.bfloat16).at[placing].set(flipped)
    out_keys = jnp.zeros((row_count,), jnp.int32).at[placing].set(inside)
    got_rows, got_keys = (
        lax.all_to_all(
            outgoing.reshape(stripe_count, bucket_rows, trait_count),
            "stripe",
            split_axis=0,
            concat_axis=0,
            tiled=True,
        ),
        lax.all_to_all(
            out_keys.reshape(stripe_count, bucket_rows),
            "stripe",
            split_axis=0,
            concat_axis=0,
            tiled=True,
        ),
    )
    aligned = (
        jnp.zeros((row_count, trait_count), jnp.bfloat16)
        .at[got_keys.reshape(row_count)]
        .set(got_rows.reshape(row_count, trait_count))
    )
    own_weight = precision[0]
    weighted = (jnp.sqrt(own_weight)[:, None] * aligned).astype(jnp.bfloat16)
    total_weight = lax.psum(own_weight, "cohort")
    received = lax.all_to_all(weighted, "cohort", split_axis=1, concat_axis=1, tiled=True)
    summed = jnp.sum(
        received.reshape(row_count, cohort_count, block_traits).astype(jnp.float32), axis=1
    )
    combined = (summed.T / jnp.sqrt(total_weight)[None, :]).astype(jnp.bfloat16)
    joined = jnp.concatenate([reference_panel, combined], axis=0)
    moved = passed_along(joined, "stripe", -1)
    panel_rim = moved[:person_count]
    score_rim = moved[person_count:]
    panel_ext = jnp.concatenate([reference_panel, panel_rim], axis=1)
    score_ext = jnp.concatenate([combined, score_rim], axis=1)

    def weight_block(gene, block, size):
        offset = block * step_width
        piece = lax.dynamic_slice(
            gene_weights[gene], (jnp.int32(0), offset), (tissue_count, step_width)
        )
        keep = offset + jnp.arange(step_width, dtype=jnp.int32) < size
        return jnp.where(keep[None, :], piece, jnp.zeros_like(piece))

    def window_variance(gene, size):
        begin = window_start[gene] - first_variant

        def add_block(block, running):
            columns = lax.dynamic_slice(
                panel_ext, (jnp.int32(0), begin + block * step_width), (person_count, step_width)
            )
            piece = weight_block(gene, block, size)
            return running + lax.dot_general(
                columns, piece, (((1,), (1,)), ((), ())), preferred_element_type=jnp.float32
            )

        blocks_needed = (size + step_width - 1) // step_width
        projected = lax.fori_loop(
            0, blocks_needed, add_block, jnp.zeros((person_count, tissue_count), jnp.float32)
        )
        return jnp.sum(projected * projected, axis=0) / person_count

    def window_score(gene):
        begin = window_start[gene] - first_variant
        size = window_length[gene]

        def add_block(block, running):
            window = lax.dynamic_slice(
                score_ext, (jnp.int32(0), begin + block * step_width), (block_traits, step_width)
            )
            piece = weight_block(gene, block, size)
            return running + lax.dot_general(
                piece, window, (((1,), (1,)), ((), ())), preferred_element_type=jnp.float32
            )

        blocks_needed = (size + step_width - 1) // step_width
        return lax.fori_loop(
            0, blocks_needed, add_block, jnp.zeros((tissue_count, block_traits), jnp.float32)
        )

    empty = jnp.zeros((gene_count, tissue_count), jnp.float32)

    def every_gene(gene, partial_value):
        return partial_value.at[gene].set(window_variance(gene, window_length[gene]))

    variance = lax.fori_loop(0, gene_count, every_gene, empty)

    def score_gene(gene, partial_value):
        return partial_value.at[gene].set(window_score(gene))

    numerator = lax.fori_loop(
        0, gene_count, score_gene, jnp.zeros((gene_count, tissue_count, block_traits), jnp.float32)
    )
    return numerator / jnp.sqrt(variance + EPSILON)[:, :, None]

MESH = pl.DeviceIdType.MESH
BF16 = jnp.bfloat16
F32 = jnp.float32
I32 = jnp.int32
Y_COUNT = 2
STRIPES = 4
HALVES = 2
CHUNKS = 6
BIN_ROWS = 64
ABSENT = -1024.0
PIECES = 3
TURNS = 2
LAG = 2


def spread_column(row):
    return jnp.transpose(jnp.broadcast_to(row, (128, 128)))


def iota(shape, dim):
    return lax.broadcasted_iota(I32, shape, dim)


def one_kernel(
    z_count,
    traits,
    persons,
    window_ref,
    size_ref,
    match_ref,
    flip_ref,
    precision_ref,
    scores_hbm,
    panel_hbm,
    weights_hbm,
    out_ref,
    scores,
    panel,
    panel_rim,
    weights,
    hot_bin,
    bin_row,
    place_row,
    slot_row,
    sign_row,
    count_total,
    enc,
    base,
    base_row,
    got_enc,
    got_base,
    starts,
    packed,
    got_first,
    got_second,
    own,
    y_got,
    pair,
    z_got,
    mine,
    rim,
    precisions,
    root,
    panel_turned,
    score_turned,
    scored,
    total_root,
    projected,
    square_row,
    squares,
    in_sem,
    rim_send,
    rim_recv,
    e_send,
    e_recv,
    b_send,
    b_recv,
    start_sem,
    x_send,
    x_recv,
    y_send,
    y_recv,
    z_send,
    z_recv,
    w_send,
    w_recv,
    s_send,
    s_recv,
    p_send,
    p_recv,
):
    cohort = lax.axis_index("cohort")
    stripe = lax.axis_index("stripe")
    cohorts = z_count * Y_COUNT
    z, y = cohort // Y_COUNT, lax.rem(cohort, Y_COUNT)
    x, core = stripe // 2, lax.rem(stripe, 2)
    rows = match_ref.shape[1]
    bucket = rows // STRIPES
    piece = bucket // PIECES
    bins = rows // 128
    width = rows // CHUNKS
    half = traits // HALVES
    part = half // cohorts
    share = panel.shape[0]
    genes = window_ref.shape[0]
    lines = weights.shape[0]
    got = (got_first, got_second)

    def partner(e):
        return lax.rem(x + e // 2, 2) * 2 + lax.rem(core + e, 2)

    scores_in = pltpu.make_async_copy(scores_hbm, scores, in_sem.at[0])
    panel_in = pltpu.make_async_copy(
        panel_hbm.at[pl.ds(pl.multiple_of(cohort * share, share), share)], panel, in_sem.at[1]
    )
    weights_in = pltpu.make_async_copy(weights_hbm, weights, in_sem.at[2])
    scores_in.start()
    panel_in.start()
    weights_in.start()

    barrier = pltpu.get_barrier_semaphore()
    for d in range(1, cohorts):
        pl.semaphore_signal(
            barrier, inc=1, device_id=(lax.rem(cohort + d, cohorts), stripe), device_id_type=MESH
        )
    for e in range(1, STRIPES):
        pl.semaphore_signal(barrier, inc=1, device_id=(cohort, partner(e)), device_id_type=MESH)

    def panel_copy():
        return pltpu.make_async_remote_copy(
            src_ref=panel,
            dst_ref=panel_rim,
            send_sem=p_send,
            recv_sem=p_recv,
            device_id=(cohort, lax.rem(stripe + STRIPES - 1, STRIPES)),
            device_id_type=MESH,
        )

    def precision_copy(d):
        return pltpu.make_async_remote_copy(
            src_ref=precision_ref,
            dst_ref=precisions.at[d],
            send_sem=w_send.at[d],
            recv_sem=w_recv.at[d],
            device_id=(lax.rem(cohort + d, cohorts), stripe),
            device_id_type=MESH,
        )

    def square_copy(d):
        return pltpu.make_async_remote_copy(
            src_ref=square_row,
            dst_ref=squares.at[d],
            send_sem=s_send.at[d],
            recv_sem=s_recv.at[d],
            device_id=(lax.rem(cohort + d, cohorts), stripe),
            device_id_type=MESH,
        )

    def enc_copy(e):
        there = pl.ds(pl.multiple_of(partner(e) * BIN_ROWS, BIN_ROWS), BIN_ROWS)
        return pltpu.make_async_remote_copy(
            src_ref=enc.at[there],
            dst_ref=got_enc.at[e],
            send_sem=e_send.at[e],
            recv_sem=e_recv.at[e],
            device_id=(cohort, partner(e)),
            device_id_type=MESH,
        )

    def base_copy(e):
        return pltpu.make_async_remote_copy(
            src_ref=base_row,
            dst_ref=got_base.at[e],
            send_sem=b_send.at[e],
            recv_sem=b_recv.at[e],
            device_id=(cohort, partner(e)),
            device_id_type=MESH,
        )

    def x_copy(h, e, p):
        here = pl.ds(p * (piece // 128), piece // 128)
        return pltpu.make_async_remote_copy(
            src_ref=packed.at[h, e, here],
            dst_ref=got[h].at[e, here],
            send_sem=x_send.at[h, e, p],
            recv_sem=x_recv.at[h, e, p],
            device_id=(cohort, partner(e)),
            device_id_type=MESH,
        )

    def y_copy(h, k):
        return pltpu.make_async_remote_copy(
            src_ref=own.at[h, k, 1 - y],
            dst_ref=y_got.at[h, k],
            send_sem=y_send.at[h, k],
            recv_sem=y_recv.at[h, k],
            device_id=(z * Y_COUNT + 1 - y, stripe),
            device_id_type=MESH,
        )

    def z_copy(h, k, d):
        other = lax.rem(z + d, z_count)
        return pltpu.make_async_remote_copy(
            src_ref=pair.at[h, k, other],
            dst_ref=z_got.at[h, k, d],
            send_sem=z_send.at[h, k, d],
            recv_sem=z_recv.at[h, k, d],
            device_id=(other * Y_COUNT + y, stripe),
            device_id_type=MESH,
        )

    def rim_copy(h, k):
        return pltpu.make_async_remote_copy(
            src_ref=mine.at[h, k],
            dst_ref=rim.at[h, k],
            send_sem=rim_send.at[h, k],
            recv_sem=rim_recv.at[h, k],
            device_id=(cohort, lax.rem(stripe + STRIPES - 1, STRIPES)),
            device_id_type=MESH,
        )

    match = match_ref[...]
    owner = jnp.zeros_like(match)
    for s in range(1, STRIPES):
        owner = owner + jnp.where(match >= s * rows, 1, 0)
    inside = match - owner * rows
    bin_row[...] = owner * BIN_ROWS + lax.shift_right_logical(inside, 7)
    place_row[...] = jnp.bitwise_and(inside, 127)
    sign_row[...] = (1 - 2 * flip_ref[...]).astype(F32)
    root[...] = jnp.sqrt(precision_ref[...])
    pl.semaphore_wait(barrier, cohorts + STRIPES - 2)
    panel_in.wait()

    @pl.when(stripe > 0)
    def _():
        panel_copy().start()

    for d in range(1, cohorts):
        precision_copy(d).start()
    bin_count = STRIPES * BIN_ROWS
    span = 512
    count_total[...] = jnp.zeros_like(count_total)
    base[...] = jnp.zeros_like(base)

    def count(c, carry):
        here = pl.ds(pl.multiple_of(c * span, span), span)
        hot = jnp.where(bin_row[:, here] == iota((bin_count, span), 0), 1.0, 0.0).astype(BF16)
        low = jnp.where(place_row[:, here] == iota((128, span), 0), 1.0, 0.0).astype(BF16)
        hot_bin[:, here] = hot
        below = jnp.where(bin_row[:, here] < iota((bin_count, span), 0), 1, 0)
        for b in range(span // 128):
            base[...] += below[:, b * 128 : (b + 1) * 128]
        count_total[...] += lax.dot_general(
            low, hot, (((1,), (1,)), ((), ())), preferred_element_type=F32
        )
        return carry

    lax.fori_loop(0, rows // span, count, 0)

    present = count_total[...]
    present16 = present.astype(BF16)
    before = jnp.where(iota((128, 128), 1) < iota((128, 128), 0), 1.0, 0.0).astype(BF16)
    within = jnp.dot(before, present16, preferred_element_type=F32)
    sums = jnp.dot(jnp.ones((128, 128), BF16), present16, preferred_element_type=F32)
    earlier = jnp.where(
        iota((bin_count, bin_count), 0) < iota((bin_count, bin_count), 1), 1.0, 0.0
    ).astype(BF16)
    first = jnp.dot(sums.astype(BF16), earlier, preferred_element_type=F32)
    coded = jnp.where(present > 0.5, within, ABSENT)
    for b in range(bin_count // 128):
        here = slice(b * 128, (b + 1) * 128)
        base_row[:, here] = jnp.sum(
            jnp.transpose(base[here, :]), axis=0, keepdims=True
        ) - bucket * lax.shift_right_logical(
            iota((1, 128), 1) + b * 128, BIN_ROWS.bit_length() - 1
        )
    for b in range(bin_count // 128):
        enc[b * 128 : (b + 1) * 128] = jnp.transpose(coded[:, b * 128 : (b + 1) * 128])
    for e in range(1, STRIPES):
        enc_copy(e).start()
        base_copy(e).start()
    mine_rows = pl.ds(pl.multiple_of(stripe * BIN_ROWS, BIN_ROWS), BIN_ROWS)
    got_enc[0] = enc[mine_rows, :]
    got_base[0] = base_row[...]
    high = jnp.floor(first[0:8] * (1.0 / 64.0))
    table = jnp.concatenate([within, high, first[0:8] - 64.0 * high], axis=0).astype(BF16)

    lane = iota((traits, traits), 1)
    source = (
        (lane % half // part % z_count * Y_COUNT + lane % half // (half // Y_COUNT))
        * (traits // cohorts)
        + lane // half * part
        + lane % part
    )
    order = jnp.where(iota((traits, traits), 0) == source, 1.0, 0.0).astype(BF16)
    scores_in.wait()

    def rank(c, carry):
        here = pl.ds(pl.multiple_of(c * span, span), span)
        found = jnp.dot(table, hot_bin[:, here], preferred_element_type=F32)
        chosen = jnp.where(place_row[:, here] == iota((128, span), 0), found[:128], 0.0)
        slot_row[:, here] = (
            jnp.sum(chosen, axis=0, keepdims=True) + 64.0 * found[128:129] + found[136:137]
        )
        scores[here, :] = jnp.dot(
            scores[here, :], order, preferred_element_type=F32
        ).astype(BF16)
        return carry

    lax.fori_loop(0, rows // span, rank, 0)

    def place_rows(e, first, blocks):
        low = (partner(e) * bucket + first * 128).astype(F32)
        size = blocks * 128
        total = jnp.zeros((size, traits), F32)
        for q in range(PIECES):
            here = slice(q * (rows // PIECES), (q + 1) * (rows // PIECES))
            hot = jnp.where(
                slot_row[:, here] - low == iota((size, rows // PIECES), 0).astype(F32),
                sign_row[:, here],
                0.0,
            ).astype(BF16)
            total = total + jnp.dot(hot, scores[here, :], preferred_element_type=F32)
        for b in range(blocks):
            for h in range(HALVES):
                packed[h, e, first + b] = jnp.transpose(
                    total[b * 128 : (b + 1) * 128, h * half : (h + 1) * half]
                ).astype(BF16)

    def pack(c, carry):
        e, p = STRIPES - 1 - c // PIECES, lax.rem(c, PIECES)
        place_rows(e, p * (piece // 128), piece // 128)

        @pl.when(e > 0)
        def _():
            x_copy(0, e, p).start()

        return carry

    lax.fori_loop(0, STRIPES * PIECES, pack, 0)
    for e in (3, 2, 1):
        for p in range(PIECES):
            x_copy(1, e, p).start()

    def turn_panel(side, offset, k):
        for b in range(width // 128):
            here = pl.multiple_of(k * width + b * 128, 128)
            block = side[:, pl.ds(here, 128)].astype(F32)
            panel_turned[pl.ds(pl.multiple_of(offset + here, 128), 128), :] = jnp.transpose(
                jnp.concatenate([block] * (128 // share), axis=0)
            )

    @pl.when(stripe < STRIPES - 1)
    def _():
        panel_copy().wait_recv()

    for e in range(1, STRIPES):
        enc_copy(e).wait_recv()
        base_copy(e).wait_recv()
    starts_in = pltpu.make_async_copy(got_base, starts, start_sem)
    starts_in.start()
    starts_in.wait()

    def align(h, k):
        for b in range(width // 128):
            at = k * (width // 128) + b
            hots, lefts = [], []
            for e in range(STRIPES):
                low = starts[e, 0, stripe * BIN_ROWS + at]
                q = jnp.minimum(lax.shift_right_logical(low, 7), bucket // 128 - 2)
                want = got_enc[e, pl.ds(at, 1), :] + (low - q * 128).astype(F32)
                hots.append(
                    jnp.where(want == iota((256, 128), 0).astype(F32), 1.0, 0.0).astype(BF16)
                )
                for step in range(2):
                    lefts.append(got[h][e, q + step] if e else packed[h, e, q + step])
            total = jnp.dot(
                jnp.concatenate(lefts, axis=1),
                jnp.concatenate(hots, axis=0),
                preferred_element_type=F32,
            )
            scaled = (total * root[:, pl.ds(pl.multiple_of(at * 128, 128), 128)]).astype(BF16)
            for yy in range(Y_COUNT):
                own[h, k, yy, :, b * 128 : (b + 1) * 128] = scaled[
                    yy * (half // 2) : (yy + 1) * (half // 2)
                ]
        y_copy(h, k).start()

    def pair_up(h, k):
        y_copy(h, k).wait_recv()
        both = own[h, k, y].astype(F32) + y_got[h, k].astype(F32)
        for zi in range(z_count):
            pair[h, k, zi] = both[zi * part : (zi + 1) * part].astype(BF16)
        for d in range(1, z_count):
            z_copy(h, k, d).start()

    def windows(side, k, first_gene, lanes_each):
        tiles = []
        place = iota((width, 128), 0) + k * width
        group = iota((1, 128), 1) // lanes_each
        count = 128 // lanes_each
        for u in range(2):
            value = None
            limit = jnp.zeros((1, 128), I32)
            for j in range(count):
                gene = first_gene + u * count + j
                piece_ = side[pl.ds(jnp.clip(window_ref[gene] - stripe * rows, 0, rows) + k * width, width), :]
                value = piece_ if j == 0 else jnp.where(group == j, piece_, value)
                limit = jnp.where(group == j, size_ref[gene], limit)
            tiles.append(jnp.where(place < limit, value, 0.0).astype(BF16))
        return jnp.concatenate(tiles, axis=1)

    def left(k):
        return weights[:, pl.ds(pl.multiple_of(k * width, width), width)]

    each = 128 // share * 2

    groups = genes // each

    def project(unit, count):
        for c in range(count):
            n = lax.rem(unit + c, groups)
            k = (unit + c) // groups
            projected[n] += jnp.dot(
                left(k), windows(panel_turned, k, n * each, share), preferred_element_type=F32
            )

    def finish(h, k):
        summed = pair[h, k, z].astype(F32)
        for d in range(1, z_count):
            z_copy(h, k, d).wait_recv()
            summed = summed + z_got[h, k, d].astype(F32)
        here = pl.ds(pl.multiple_of(k * width, width), width)
        mine[h, k] = (summed / total_root[:, here]).astype(BF16)

        @pl.when(stripe > 0)
        def _():
            rim_copy(h, k).start()

    def turn_scores(side, h, k, offset):
        for b in range(width // 128):
            block = side[h, k, :, b * 128 : (b + 1) * 128].astype(F32)
            score_turned[
                h, pl.ds(pl.multiple_of(offset + k * width + b * 128, 128), 128), :
            ] = jnp.transpose(jnp.concatenate([block] * (128 // part), axis=0))

    def score(h, k):
        scored[h] += jnp.dot(
            left(k), windows(score_turned.at[h], k, 0, part), preferred_element_type=F32
        )

    def rim_in(h):
        def one(k, carry):
            @pl.when(stripe < STRIPES - 1)
            def _():
                rim_copy(h, k).wait_recv()

            turn_scores(rim, h, k, rows)
            return carry

        lax.fori_loop(0, CHUNKS, one, 0)

    for e in range(1, STRIPES):
        for p in range(PIECES):
            x_copy(0, e, p).wait_recv()

    def first_half(k, carry):
        @pl.when(k < CHUNKS)
        def _():
            align(0, k)

        @pl.when(k < TURNS)
        def _():
            for c in range(CHUNKS // TURNS):
                turn_panel(panel, 0, k * (CHUNKS // TURNS) + c)
                turn_panel(panel_rim, rows, k * (CHUNKS // TURNS) + c)

        @pl.when(k == TURNS)
        def _():
            weights_in.wait()
            projected[...] = jnp.zeros_like(projected)

        @pl.when(k >= TURNS)
        def _():
            project(2 * (k - TURNS), 2)

        @pl.when(k >= LAG)
        def _():
            pair_up(0, k - LAG)

        return carry

    lax.fori_loop(0, CHUNKS + LAG, first_half, 0)
    precision_sum = precision_ref[...]
    for d in range(1, cohorts):
        precision_copy(d).wait_recv()
        precision_sum = precision_sum + precisions[d]
    total_root[...] = jnp.sqrt(precision_sum)
    scored[...] = jnp.zeros_like(scored)

    for e in range(1, STRIPES):
        for p in range(PIECES):
            x_copy(1, e, p).wait_recv()

    def second_half(k, carry):
        @pl.when(k < CHUNKS)
        def _():
            align(1, k)

        @pl.when(k < 3)
        def _():
            for c in range(2):
                finish(0, 2 * k + c)
                turn_scores(mine, 0, 2 * k + c, 0)

        @pl.when(k < 4)
        def _():
            project(12 + 3 * k, 3)

        @pl.when(k == 3)
        def _():
            rim_in(0)

        @pl.when(jnp.logical_and(k > 3, k < 7))
        def _():
            for c in range(2):
                score(0, 2 * (k - 4) + c)

        @pl.when(k >= LAG)
        def _():
            pair_up(1, k - LAG)

        return carry

    lax.fori_loop(0, CHUNKS + LAG, second_half, 0)

    line_gene = jnp.bitwise_and(iota((lines, 1), 0), genes - 1)
    square = jnp.zeros((lines, 128), F32)
    for n in range(genes // each):
        for u in range(2):
            value = projected[n, :, u * 128 : (u + 1) * 128]
            gene = n * each + u * (each // 2) + iota((1, 128), 1) // share
            square = square + jnp.where(line_gene == gene, value * value, 0.0)
    blocks = square_row.shape[0]
    square = jnp.concatenate([square, jnp.zeros((blocks * 128 - lines, 128), F32)], axis=0)
    for b in range(blocks):
        square_row[b : b + 1, :] = jnp.sum(
            jnp.transpose(square[b * 128 : (b + 1) * 128]), axis=0, keepdims=True
        )
    for d in range(1, cohorts):
        square_copy(d).start()

    def last(k, carry):
        finish(1, k)
        turn_scores(mine, 1, k, 0)
        return carry

    lax.fori_loop(0, CHUNKS, last, 0)

    square_sum = square_row[...]
    for d in range(1, cohorts):
        square_copy(d).wait_recv()
        square_sum = square_sum + squares[d]
    spread = 1.0 / jnp.sqrt(square_sum / persons + EPSILON)
    scale = jnp.concatenate([spread_column(spread[b : b + 1]) for b in range(blocks)], axis=0)
    rim_in(1)

    def score_last(k, carry):
        score(1, k)
        return carry

    lax.fori_loop(0, CHUNKS, score_last, 0)
    folded = []
    for h in range(HALVES):
        total = jnp.zeros((lines, 128), F32)
        for u in range(2):
            gene = u * (genes // 2) + iota((1, 128), 1) // part
            total = total + jnp.where(
                line_gene == gene, scored[h, :, u * 128 : (u + 1) * 128], 0.0
            )
        for turn in (64, 32, 16):
            total = total + pltpu.roll(total, turn, 1)
        folded.append(total)
    total = jnp.where(iota((1, 128), 1) < part, folded[0], folded[1])
    out_ref[...] = (total * scale[:lines])[:, : HALVES * part]

    for h in range(HALVES):
        for k in range(CHUNKS):
            y_copy(h, k).wait_send()
            for d in range(1, z_count):
                z_copy(h, k, d).wait_send()

            @pl.when(stripe > 0)
            def _():
                rim_copy(h, k).wait_send()

        for e in range(1, STRIPES):
            for p in range(PIECES):
                x_copy(h, e, p).wait_send()
    for e in range(1, STRIPES):
        enc_copy(e).wait_send()
        base_copy(e).wait_send()
    for d in range(1, cohorts):
        precision_copy(d).wait_send()
        square_copy(d).wait_send()

    @pl.when(stripe > 0)
    def _():
        panel_copy().wait_send()


def fast_device(
    cohort_scores,
    allele_match,
    allele_flip,
    precision,
    reference_panel,
    gene_weights,
    window_start,
    window_length,
):
    rows, traits = cohort_scores.shape[1:]
    cohorts = lax.axis_size("cohort")
    z_count = cohorts // Y_COUNT
    bucket = rows // STRIPES
    persons = reference_panel.shape[0]
    share = persons // cohorts
    genes, tissues, span = gene_weights.shape
    lines = genes * tissues
    width = rows // CHUNKS
    half = traits // HALVES
    part = half // cohorts
    blocks = -(-lines // 1024) * 8
    vmem = pl.BlockSpec(memory_space=pltpu.VMEM)
    smem = pl.BlockSpec(memory_space=pltpu.SMEM)
    hbm = pl.BlockSpec(memory_space=pl.ANY)
    dma = pltpu.SemaphoreType.DMA
    table = pl.pallas_call(
        functools.partial(one_kernel, z_count, traits, persons),
        out_shape=jax.ShapeDtypeStruct((lines, HALVES * part), F32),
        in_specs=[smem, smem, vmem, vmem, vmem, hbm, hbm, hbm],
        out_specs=vmem,
        scratch_shapes=[
            pltpu.VMEM((rows, traits), BF16),
            pltpu.VMEM((share, rows), BF16),
            pltpu.VMEM((share, rows), BF16),
            pltpu.VMEM((lines, span), BF16),
            pltpu.VMEM((STRIPES * BIN_ROWS, rows), BF16),
            pltpu.VMEM((1, rows), I32),
            pltpu.VMEM((1, rows), I32),
            pltpu.VMEM((1, rows), F32),
            pltpu.VMEM((1, rows), F32),
            pltpu.VMEM((128, STRIPES * BIN_ROWS), F32),
            pltpu.VMEM((STRIPES * BIN_ROWS, 128), F32),
            pltpu.VMEM((STRIPES * BIN_ROWS, 128), I32),
            pltpu.VMEM((1, STRIPES * BIN_ROWS), I32),
            pltpu.VMEM((STRIPES, BIN_ROWS, 128), F32),
            pltpu.VMEM((STRIPES, 1, STRIPES * BIN_ROWS), I32),
            pltpu.SMEM((STRIPES, 1, STRIPES * BIN_ROWS), I32),
            pltpu.VMEM((HALVES, STRIPES, bucket // 128, half, 128), BF16),
            pltpu.VMEM((STRIPES, bucket // 128, half, 128), BF16),
            pltpu.VMEM((STRIPES, bucket // 128, half, 128), BF16),
            pltpu.VMEM((HALVES, CHUNKS, Y_COUNT, half // 2, width), BF16),
            pltpu.VMEM((HALVES, CHUNKS, half // 2, width), BF16),
            pltpu.VMEM((HALVES, CHUNKS, z_count, part, width), BF16),
            pltpu.VMEM((HALVES, CHUNKS, z_count, part, width), BF16),
            pltpu.VMEM((HALVES, CHUNKS, part, width), BF16),
            pltpu.VMEM((HALVES, CHUNKS, part, width), BF16),
            pltpu.VMEM((cohorts, 1, rows), F32),
            pltpu.VMEM((1, rows), F32),
            pltpu.VMEM((2 * rows, 128), F32),
            pltpu.VMEM((HALVES, 2 * rows, 128), F32),
            pltpu.VMEM((HALVES, lines, 256), F32),
            pltpu.VMEM((1, rows), F32),
            pltpu.VMEM((genes * share // 256, lines, 256), F32),
            pltpu.VMEM((blocks, 128), F32),
            pltpu.VMEM((cohorts, blocks, 128), F32),
            dma((3,)),
            dma((HALVES, CHUNKS)),
            dma((HALVES, CHUNKS)),
            dma((STRIPES,)),
            dma((STRIPES,)),
            dma((STRIPES,)),
            dma((STRIPES,)),
            dma,
            dma((HALVES, STRIPES, PIECES)),
            dma((HALVES, STRIPES, PIECES)),
            dma((HALVES, CHUNKS)),
            dma((HALVES, CHUNKS)),
            dma((HALVES, CHUNKS, z_count)),
            dma((HALVES, CHUNKS, z_count)),
            dma((cohorts,)),
            dma((cohorts,)),
            dma((cohorts,)),
            dma((cohorts,)),
            dma,
            dma,
        ],
        compiler_params=pltpu.CompilerParams(
            collective_id=0, has_side_effects=True, vmem_limit_bytes=58 * 2**20
        ),
    )(
        window_start,
        window_length,
        allele_match,
        allele_flip,
        precision,
        cohort_scores[0],
        reference_panel,
        jnp.transpose(gene_weights, (1, 0, 2)).reshape(lines, span),
    )
    return jnp.transpose(table.reshape(tissues, genes, HALVES * part), (1, 0, 2))


def on_device(cohort_scores, *others):
    rows, traits = cohort_scores.shape[1:]
    stripes = lax.axis_size("stripe")
    cohorts = lax.axis_size("cohort")
    persons = others[3].shape[0]
    genes, tissues, span = others[4].shape
    fits = (
        stripes == STRIPES
        and cohorts == 8
        and traits == 256
        and genes == 16
        and persons == 64 * cohorts
        and rows % (128 * PIECES * STRIPES) == 0
        and rows % (128 * CHUNKS) == 0
        and rows % 512 == 0
        and rows // 128 <= BIN_ROWS
        and rows // STRIPES >= 256
        and span == rows
        and tissues * genes <= 1024
    )
    if fits:
        return fast_device(cohort_scores, *others)
    return general_device(cohort_scores, *others)


def solution(mesh):
    in_specs = (
        P("cohort", "stripe", None),
        P("cohort", "stripe"),
        P("cohort", "stripe"),
        P("cohort", "stripe"),
        P(None, "stripe"),
        P("stripe", None, None),
        P("stripe"),
        P("stripe"),
    )
    out_specs = P("stripe", None, "cohort")
    return jax.shard_map(
        on_device, mesh=mesh, in_specs=in_specs, out_specs=out_specs, check_vma=False
    )
```

```python
import functools

import jax
import jax.numpy as jnp
from jax import lax
from jax.experimental import pallas as pl
from jax.experimental.pallas import tpu as pltpu
from jax.sharding import PartitionSpec as P

EPSILON = 1e-06


def passed_along(block, axis, distance):
    devices = range(lax.axis_size(axis))
    route = [(i - distance, i) for i in devices if i - distance in devices]
    return lax.ppermute(block, axis, route)


def running_count(member):
    rows, columns = member.shape
    block = 128 if rows % 128 == 0 else rows
    parts = member.astype(jnp.float32).reshape(rows // block, block, columns)
    inner = jnp.einsum(
        "ij,bjc->bic",
        jnp.tril(jnp.ones((block, block), jnp.float32)),
        parts,
        precision=lax.Precision.HIGHEST,
    )
    outer = jnp.einsum(
        "ab,bc->ac",
        jnp.tril(jnp.ones((rows // block, rows // block), jnp.float32), -1),
        inner[:, -1, :],
        precision=lax.Precision.HIGHEST,
    )
    return (inner + outer[:, None, :]).reshape(rows, columns).astype(jnp.int32)


def general_device(
    cohort_scores,
    allele_match,
    allele_flip,
    precision,
    reference_panel,
    gene_weights,
    window_start,
    window_length,
):
    row_count = cohort_scores.shape[1]
    trait_count = cohort_scores.shape[2]
    stripe_count = lax.axis_size("stripe")
    cohort_count = lax.axis_size("cohort")
    bucket_rows = row_count // stripe_count
    block_traits = trait_count // cohort_count
    person_count = reference_panel.shape[0]
    gene_count = gene_weights.shape[0]
    tissue_count = gene_weights.shape[1]
    window_span = gene_weights.shape[2]
    step_width = min(512, window_span)
    first_variant = lax.axis_index("stripe") * row_count
    target = allele_match[0] // row_count
    inside = allele_match[0] - target * row_count
    member = (target[:, None] == jnp.arange(stripe_count, dtype=jnp.int32)[None, :]).astype(
        jnp.int32
    )
    ranking = jnp.sum(running_count(member) * member, axis=1) - 1
    placing = target * bucket_rows + ranking
    signs = (1 - 2 * allele_flip[0]).astype(jnp.bfloat16)
    flipped = cohort_scores[0] * signs[:, None]
    outgoing = jnp.zeros((row_count, trait_count), jnp.bfloat16).at[placing].set(flipped)
    out_keys = jnp.zeros((row_count,), jnp.int32).at[placing].set(inside)
    got_rows, got_keys = (
        lax.all_to_all(
            outgoing.reshape(stripe_count, bucket_rows, trait_count),
            "stripe",
            split_axis=0,
            concat_axis=0,
            tiled=True,
        ),
        lax.all_to_all(
            out_keys.reshape(stripe_count, bucket_rows),
            "stripe",
            split_axis=0,
            concat_axis=0,
            tiled=True,
        ),
    )
    aligned = (
        jnp.zeros((row_count, trait_count), jnp.bfloat16)
        .at[got_keys.reshape(row_count)]
        .set(got_rows.reshape(row_count, trait_count))
    )
    own_weight = precision[0]
    weighted = (jnp.sqrt(own_weight)[:, None] * aligned).astype(jnp.bfloat16)
    total_weight = lax.psum(own_weight, "cohort")
    received = lax.all_to_all(weighted, "cohort", split_axis=1, concat_axis=1, tiled=True)
    summed = jnp.sum(
        received.reshape(row_count, cohort_count, block_traits).astype(jnp.float32), axis=1
    )
    combined = (summed.T / jnp.sqrt(total_weight)[None, :]).astype(jnp.bfloat16)
    joined = jnp.concatenate([reference_panel, combined], axis=0)
    moved = passed_along(joined, "stripe", -1)
    panel_rim = moved[:person_count]
    score_rim = moved[person_count:]
    panel_ext = jnp.concatenate([reference_panel, panel_rim], axis=1)
    score_ext = jnp.concatenate([combined, score_rim], axis=1)

    def weight_block(gene, block, size):
        offset = block * step_width
        piece = lax.dynamic_slice(
            gene_weights[gene], (jnp.int32(0), offset), (tissue_count, step_width)
        )
        keep = offset + jnp.arange(step_width, dtype=jnp.int32) < size
        return jnp.where(keep[None, :], piece, jnp.zeros_like(piece))

    def window_variance(gene, size):
        begin = window_start[gene] - first_variant

        def add_block(block, running):
            columns = lax.dynamic_slice(
                panel_ext, (jnp.int32(0), begin + block * step_width), (person_count, step_width)
            )
            piece = weight_block(gene, block, size)
            return running + lax.dot_general(
                columns, piece, (((1,), (1,)), ((), ())), preferred_element_type=jnp.float32
            )

        blocks_needed = (size + step_width - 1) // step_width
        projected = lax.fori_loop(
            0, blocks_needed, add_block, jnp.zeros((person_count, tissue_count), jnp.float32)
        )
        return jnp.sum(projected * projected, axis=0) / person_count

    def window_score(gene):
        begin = window_start[gene] - first_variant
        size = window_length[gene]

        def add_block(block, running):
            window = lax.dynamic_slice(
                score_ext, (jnp.int32(0), begin + block * step_width), (block_traits, step_width)
            )
            piece = weight_block(gene, block, size)
            return running + lax.dot_general(
                piece, window, (((1,), (1,)), ((), ())), preferred_element_type=jnp.float32
            )

        blocks_needed = (size + step_width - 1) // step_width
        return lax.fori_loop(
            0, blocks_needed, add_block, jnp.zeros((tissue_count, block_traits), jnp.float32)
        )

    empty = jnp.zeros((gene_count, tissue_count), jnp.float32)

    def every_gene(gene, partial_value):
        return partial_value.at[gene].set(window_variance(gene, window_length[gene]))

    variance = lax.fori_loop(0, gene_count, every_gene, empty)

    def score_gene(gene, partial_value):
        return partial_value.at[gene].set(window_score(gene))

    numerator = lax.fori_loop(
        0, gene_count, score_gene, jnp.zeros((gene_count, tissue_count, block_traits), jnp.float32)
    )
    return numerator / jnp.sqrt(variance + EPSILON)[:, :, None]

MESH = pl.DeviceIdType.MESH
BF16 = jnp.bfloat16
F32 = jnp.float32
I32 = jnp.int32
Y_COUNT = 2
STRIPES = 4
HALVES = 2
CHUNKS = 6
BIN_ROWS = 64
ABSENT = -1024.0
PIECES = 3
TURNS = 2
LAG = 2
DEPTHS = 3


def spread_column(row):
    return jnp.transpose(jnp.broadcast_to(row, (128, 128)))


def iota(shape, dim):
    return lax.broadcasted_iota(I32, shape, dim)


def one_kernel(
    z_count,
    traits,
    persons,
    window_ref,
    size_ref,
    match_ref,
    flip_ref,
    precision_ref,
    scores_hbm,
    panel_hbm,
    weights_hbm,
    out_ref,
    scores,
    panel,
    panel_rim,
    weights,
    hot_bin,
    bin_row,
    place_row,
    slot_row,
    sign_row,
    count_total,
    enc,
    base,
    base_row,
    got_enc,
    got_base,
    starts,
    packed,
    got_first,
    got_second,
    own,
    y_got,
    pair,
    z_got,
    mine,
    rim,
    precisions,
    root,
    panel_turned,
    score_turned,
    scored,
    total_root,
    projected,
    square_row,
    squares,
    in_sem,
    rim_send,
    rim_recv,
    e_send,
    e_recv,
    b_send,
    b_recv,
    start_sem,
    x_send,
    x_recv,
    y_send,
    y_recv,
    z_send,
    z_recv,
    w_send,
    w_recv,
    s_send,
    s_recv,
    p_send,
    p_recv,
):
    cohort = lax.axis_index("cohort")
    stripe = lax.axis_index("stripe")
    cohorts = z_count * Y_COUNT
    z, y = cohort // Y_COUNT, lax.rem(cohort, Y_COUNT)
    x, core = stripe // 2, lax.rem(stripe, 2)
    rows = match_ref.shape[1]
    bucket = rows // STRIPES
    piece = bucket // PIECES
    bins = rows // 128
    width = rows // CHUNKS
    deep = rows // DEPTHS
    half = traits // HALVES
    part = half // cohorts
    share = panel.shape[0]
    genes = window_ref.shape[0]
    lines = weights.shape[0]
    got = (got_first, got_second)

    def partner(e):
        return lax.rem(x + e // 2, 2) * 2 + lax.rem(core + e, 2)

    scores_in = pltpu.make_async_copy(scores_hbm, scores, in_sem.at[0])
    panel_in = pltpu.make_async_copy(
        panel_hbm.at[pl.ds(pl.multiple_of(cohort * share, share), share)], panel, in_sem.at[1]
    )
    weights_in = pltpu.make_async_copy(weights_hbm, weights, in_sem.at[2])
    scores_in.start()
    panel_in.start()
    weights_in.start()

    barrier = pltpu.get_barrier_semaphore()
    for d in range(1, cohorts):
        pl.semaphore_signal(
            barrier, inc=1, device_id=(lax.rem(cohort + d, cohorts), stripe), device_id_type=MESH
        )
    for e in range(1, STRIPES):
        pl.semaphore_signal(barrier, inc=1, device_id=(cohort, partner(e)), device_id_type=MESH)

    def panel_copy():
        return pltpu.make_async_remote_copy(
            src_ref=panel,
            dst_ref=panel_rim,
            send_sem=p_send,
            recv_sem=p_recv,
            device_id=(cohort, lax.rem(stripe + STRIPES - 1, STRIPES)),
            device_id_type=MESH,
        )

    def precision_copy(d):
        return pltpu.make_async_remote_copy(
            src_ref=precision_ref,
            dst_ref=precisions.at[d],
            send_sem=w_send.at[d],
            recv_sem=w_recv.at[d],
            device_id=(lax.rem(cohort + d, cohorts), stripe),
            device_id_type=MESH,
        )

    def square_copy(d):
        return pltpu.make_async_remote_copy(
            src_ref=square_row,
            dst_ref=squares.at[d],
            send_sem=s_send.at[d],
            recv_sem=s_recv.at[d],
            device_id=(lax.rem(cohort + d, cohorts), stripe),
            device_id_type=MESH,
        )

    def enc_copy(e):
        there = pl.ds(pl.multiple_of(partner(e) * BIN_ROWS, BIN_ROWS), BIN_ROWS)
        return pltpu.make_async_remote_copy(
            src_ref=enc.at[there],
            dst_ref=got_enc.at[e],
            send_sem=e_send.at[e],
            recv_sem=e_recv.at[e],
            device_id=(cohort, partner(e)),
            device_id_type=MESH,
        )

    def base_copy(e):
        return pltpu.make_async_remote_copy(
            src_ref=base_row,
            dst_ref=got_base.at[e],
            send_sem=b_send.at[e],
            recv_sem=b_recv.at[e],
            device_id=(cohort, partner(e)),
            device_id_type=MESH,
        )

    def x_copy(h, e, p):
        here = pl.ds(p * (piece // 128), piece // 128)
        return pltpu.make_async_remote_copy(
            src_ref=packed.at[h, e, here],
            dst_ref=got[h].at[e, here],
            send_sem=x_send.at[h, e, p],
            recv_sem=x_recv.at[h, e, p],
            device_id=(cohort, partner(e)),
            device_id_type=MESH,
        )

    def y_copy(h, k):
        return pltpu.make_async_remote_copy(
            src_ref=own.at[h, k, 1 - y],
            dst_ref=y_got.at[h, k],
            send_sem=y_send.at[h, k],
            recv_sem=y_recv.at[h, k],
            device_id=(z * Y_COUNT + 1 - y, stripe),
            device_id_type=MESH,
        )

    def z_copy(h, k, d):
        other = lax.rem(z + d, z_count)
        return pltpu.make_async_remote_copy(
            src_ref=pair.at[h, k, other],
            dst_ref=z_got.at[h, k, d],
            send_sem=z_send.at[h, k, d],
            recv_sem=z_recv.at[h, k, d],
            device_id=(other * Y_COUNT + y, stripe),
            device_id_type=MESH,
        )

    def rim_copy(h, k):
        return pltpu.make_async_remote_copy(
            src_ref=mine.at[h, k],
            dst_ref=rim.at[h, k],
            send_sem=rim_send.at[h, k],
            recv_sem=rim_recv.at[h, k],
            device_id=(cohort, lax.rem(stripe + STRIPES - 1, STRIPES)),
            device_id_type=MESH,
        )

    match = match_ref[...]
    owner = jnp.zeros_like(match)
    for s in range(1, STRIPES):
        owner = owner + jnp.where(match >= s * rows, 1, 0)
    inside = match - owner * rows
    bin_row[...] = owner * BIN_ROWS + lax.shift_right_logical(inside, 7)
    place_row[...] = jnp.bitwise_and(inside, 127)
    sign_row[...] = (1 - 2 * flip_ref[...]).astype(F32)
    root[...] = jnp.sqrt(precision_ref[...])
    pl.semaphore_wait(barrier, cohorts + STRIPES - 2)
    panel_in.wait()

    @pl.when(stripe > 0)
    def _():
        panel_copy().start()

    for d in range(1, cohorts):
        precision_copy(d).start()
    bin_count = STRIPES * BIN_ROWS
    span = 512
    count_total[...] = jnp.zeros_like(count_total)
    base[...] = jnp.zeros_like(base)

    def count(c, carry):
        here = pl.ds(pl.multiple_of(c * span, span), span)
        hot = jnp.where(bin_row[:, here] == iota((bin_count, span), 0), 1.0, 0.0).astype(BF16)
        low = jnp.where(place_row[:, here] == iota((128, span), 0), 1.0, 0.0).astype(BF16)
        hot_bin[:, here] = hot
        below = jnp.where(bin_row[:, here] < iota((bin_count, span), 0), 1, 0)
        for b in range(span // 128):
            base[...] += below[:, b * 128 : (b + 1) * 128]
        count_total[...] += lax.dot_general(
            low, hot, (((1,), (1,)), ((), ())), preferred_element_type=F32
        )
        return carry

    lax.fori_loop(0, rows // span, count, 0)

    present = count_total[...]
    present16 = present.astype(BF16)
    before = jnp.where(iota((128, 128), 1) < iota((128, 128), 0), 1.0, 0.0).astype(BF16)
    within = jnp.dot(before, present16, preferred_element_type=F32)
    sums = jnp.dot(jnp.ones((128, 128), BF16), present16, preferred_element_type=F32)
    earlier = jnp.where(
        iota((bin_count, bin_count), 0) < iota((bin_count, bin_count), 1), 1.0, 0.0
    ).astype(BF16)
    first = jnp.dot(sums.astype(BF16), earlier, preferred_element_type=F32)
    coded = jnp.where(present > 0.5, within, ABSENT)
    for b in range(bin_count // 128):
        here = slice(b * 128, (b + 1) * 128)
        base_row[:, here] = jnp.sum(
            jnp.transpose(base[here, :]), axis=0, keepdims=True
        ) - bucket * lax.shift_right_logical(
            iota((1, 128), 1) + b * 128, BIN_ROWS.bit_length() - 1
        )
    for b in range(bin_count // 128):
        enc[b * 128 : (b + 1) * 128] = jnp.transpose(coded[:, b * 128 : (b + 1) * 128])
    for e in range(1, STRIPES):
        enc_copy(e).start()
        base_copy(e).start()
    mine_rows = pl.ds(pl.multiple_of(stripe * BIN_ROWS, BIN_ROWS), BIN_ROWS)
    got_enc[0] = enc[mine_rows, :]
    got_base[0] = base_row[...]
    high = jnp.floor(first[0:8] * (1.0 / 64.0))
    table = jnp.concatenate([within, high, first[0:8] - 64.0 * high], axis=0).astype(BF16)

    lane = iota((traits, traits), 1)
    source = (
        (lane % half // part % z_count * Y_COUNT + lane % half // (half // Y_COUNT))
        * (traits // cohorts)
        + lane // half * part
        + lane % part
    )
    order = jnp.where(iota((traits, traits), 0) == source, 1.0, 0.0).astype(BF16)
    scores_in.wait()

    def rank(c, carry):
        here = pl.ds(pl.multiple_of(c * span, span), span)
        found = jnp.dot(table, hot_bin[:, here], preferred_element_type=F32)
        chosen = jnp.where(place_row[:, here] == iota((128, span), 0), found[:128], 0.0)
        slot_row[:, here] = (
            jnp.sum(chosen, axis=0, keepdims=True) + 64.0 * found[128:129] + found[136:137]
        )
        scores[here, :] = jnp.dot(
            scores[here, :], order, preferred_element_type=F32
        ).astype(BF16)
        return carry

    lax.fori_loop(0, rows // span, rank, 0)

    def place_rows(e, first, blocks):
        low = (partner(e) * bucket + first * 128).astype(F32)
        size = blocks * 128
        total = jnp.zeros((size, traits), F32)
        for q in range(PIECES):
            here = slice(q * (rows // PIECES), (q + 1) * (rows // PIECES))
            hot = jnp.where(
                slot_row[:, here] - low == iota((size, rows // PIECES), 0).astype(F32),
                sign_row[:, here],
                0.0,
            ).astype(BF16)
            total = total + jnp.dot(hot, scores[here, :], preferred_element_type=F32)
        for b in range(blocks):
            for h in range(HALVES):
                packed[h, e, first + b] = jnp.transpose(
                    total[b * 128 : (b + 1) * 128, h * half : (h + 1) * half]
                ).astype(BF16)

    def pack(c, carry):
        e, p = STRIPES - 1 - c // PIECES, lax.rem(c, PIECES)
        place_rows(e, p * (piece // 128), piece // 128)

        @pl.when(e > 0)
        def _():
            x_copy(0, e, p).start()

        return carry

    lax.fori_loop(0, STRIPES * PIECES, pack, 0)
    for e in (3, 2, 1):
        for p in range(PIECES):
            x_copy(1, e, p).start()

    def turn_panel(side, offset, k):
        for b in range(width // 128):
            here = pl.multiple_of(k * width + b * 128, 128)
            block = side[:, pl.ds(here, 128)].astype(F32)
            panel_turned[pl.ds(pl.multiple_of(offset + here, 128), 128), :] = jnp.transpose(
                jnp.concatenate([block] * (128 // share), axis=0)
            )

    @pl.when(stripe < STRIPES - 1)
    def _():
        panel_copy().wait_recv()

    for e in range(1, STRIPES):
        enc_copy(e).wait_recv()
        base_copy(e).wait_recv()
    starts_in = pltpu.make_async_copy(got_base, starts, start_sem)
    starts_in.start()
    starts_in.wait()

    def align(h, k):
        for b in range(width // 128):
            at = k * (width // 128) + b
            hots, lefts = [], []
            for e in range(STRIPES):
                low = starts[e, 0, stripe * BIN_ROWS + at]
                q = jnp.minimum(lax.shift_right_logical(low, 7), bucket // 128 - 2)
                want = got_enc[e, pl.ds(at, 1), :] + (low - q * 128).astype(F32)
                hots.append(
                    jnp.where(want == iota((256, 128), 0).astype(F32), 1.0, 0.0).astype(BF16)
                )
                for step in range(2):
                    lefts.append(got[h][e, q + step] if e else packed[h, e, q + step])
            total = jnp.dot(
                jnp.concatenate(lefts, axis=1),
                jnp.concatenate(hots, axis=0),
                preferred_element_type=F32,
            )
            scaled = (total * root[:, pl.ds(pl.multiple_of(at * 128, 128), 128)]).astype(BF16)
            for yy in range(Y_COUNT):
                own[h, k, yy, :, b * 128 : (b + 1) * 128] = scaled[
                    yy * (half // 2) : (yy + 1) * (half // 2)
                ]
        y_copy(h, k).start()

    def pair_up(h, k):
        y_copy(h, k).wait_recv()
        both = own[h, k, y].astype(F32) + y_got[h, k].astype(F32)
        for zi in range(z_count):
            pair[h, k, zi] = both[zi * part : (zi + 1) * part].astype(BF16)
        for d in range(1, z_count):
            z_copy(h, k, d).start()

    def windows(side, k, first_gene, lanes_each):
        tiles = []
        place = iota((deep, 128), 0) + k * deep
        group = iota((1, 128), 1) // lanes_each
        count = 128 // lanes_each
        for u in range(2):
            value = None
            limit = jnp.zeros((1, 128), I32)
            for j in range(count):
                gene = first_gene + u * count + j
                piece_ = side[pl.ds(jnp.clip(window_ref[gene] - stripe * rows, 0, rows) + k * deep, deep), :]
                value = piece_ if j == 0 else jnp.where(group == j, piece_, value)
                limit = jnp.where(group == j, size_ref[gene], limit)
            tiles.append(jnp.where(place < limit, value, 0.0).astype(BF16))
        return jnp.concatenate(tiles, axis=1)

    def left(k):
        return weights[:, pl.ds(pl.multiple_of(k * deep, deep), deep)]

    each = 128 // share * 2

    groups = genes // each

    def project(unit, count):
        for c in range(count):
            n = lax.rem(unit + c, groups)
            k = (unit + c) // groups
            projected[n] += jnp.dot(
                left(k), windows(panel_turned, k, n * each, share), preferred_element_type=F32
            )

    def finish(h, k):
        summed = pair[h, k, z].astype(F32)
        for d in range(1, z_count):
            z_copy(h, k, d).wait_recv()
            summed = summed + z_got[h, k, d].astype(F32)
        here = pl.ds(pl.multiple_of(k * width, width), width)
        mine[h, k] = (summed / total_root[:, here]).astype(BF16)

        @pl.when(stripe > 0)
        def _():
            rim_copy(h, k).start()

    def turn_scores(side, h, k, offset):
        for b in range(width // 128):
            block = side[h, k, :, b * 128 : (b + 1) * 128].astype(F32)
            score_turned[
                h, pl.ds(pl.multiple_of(offset + k * width + b * 128, 128), 128), :
            ] = jnp.transpose(jnp.concatenate([block] * (128 // part), axis=0))

    def score(h, k):
        scored[h] += jnp.dot(
            left(k), windows(score_turned.at[h], k, 0, part), preferred_element_type=F32
        )

    def rim_in(h):
        def one(k, carry):
            @pl.when(stripe < STRIPES - 1)
            def _():
                rim_copy(h, k).wait_recv()

            turn_scores(rim, h, k, rows)
            return carry

        lax.fori_loop(0, CHUNKS, one, 0)

    for e in range(1, STRIPES):
        for p in range(PIECES):
            x_copy(0, e, p).wait_recv()

    def first_half(k, carry):
        @pl.when(k < CHUNKS)
        def _():
            align(0, k)

        @pl.when(k < TURNS)
        def _():
            for c in range(CHUNKS // TURNS):
                turn_panel(panel, 0, k * (CHUNKS // TURNS) + c)
                turn_panel(panel_rim, rows, k * (CHUNKS // TURNS) + c)

        @pl.when(k == TURNS)
        def _():
            weights_in.wait()
            projected[...] = jnp.zeros_like(projected)

        @pl.when(k >= TURNS)
        def _():
            project(k - TURNS, 1)

        @pl.when(k >= LAG)
        def _():
            pair_up(0, k - LAG)

        return carry

    lax.fori_loop(0, CHUNKS + LAG, first_half, 0)
    precision_sum = precision_ref[...]
    for d in range(1, cohorts):
        precision_copy(d).wait_recv()
        precision_sum = precision_sum + precisions[d]
    total_root[...] = jnp.sqrt(precision_sum)
    scored[...] = jnp.zeros_like(scored)

    for e in range(1, STRIPES):
        for p in range(PIECES):
            x_copy(1, e, p).wait_recv()

    def second_half(k, carry):
        @pl.when(k < CHUNKS)
        def _():
            align(1, k)

        @pl.when(k < 3)
        def _():
            for c in range(2):
                finish(0, 2 * k + c)
                turn_scores(mine, 0, 2 * k + c, 0)

        @pl.when(k < 3)
        def _():
            project(6 + 2 * k, 2)

        @pl.when(k == 3)
        def _():
            rim_in(0)

        @pl.when(jnp.logical_and(k > 3, k < 7))
        def _():
            score(0, k - 4)

        @pl.when(k >= LAG)
        def _():
            pair_up(1, k - LAG)

        return carry

    lax.fori_loop(0, CHUNKS + LAG, second_half, 0)

    line_gene = jnp.bitwise_and(iota((lines, 1), 0), genes - 1)
    square = jnp.zeros((lines, 128), F32)
    for n in range(genes // each):
        for u in range(2):
            value = projected[n, :, u * 128 : (u + 1) * 128]
            gene = n * each + u * (each // 2) + iota((1, 128), 1) // share
            square = square + jnp.where(line_gene == gene, value * value, 0.0)
    blocks = square_row.shape[0]
    square = jnp.concatenate([square, jnp.zeros((blocks * 128 - lines, 128), F32)], axis=0)
    for b in range(blocks):
        square_row[b : b + 1, :] = jnp.sum(
            jnp.transpose(square[b * 128 : (b + 1) * 128]), axis=0, keepdims=True
        )
    for d in range(1, cohorts):
        square_copy(d).start()

    def last(k, carry):
        finish(1, k)
        turn_scores(mine, 1, k, 0)
        return carry

    lax.fori_loop(0, CHUNKS, last, 0)

    square_sum = square_row[...]
    for d in range(1, cohorts):
        square_copy(d).wait_recv()
        square_sum = square_sum + squares[d]
    spread = 1.0 / jnp.sqrt(square_sum / persons + EPSILON)
    scale = jnp.concatenate([spread_column(spread[b : b + 1]) for b in range(blocks)], axis=0)
    rim_in(1)

    for k in range(DEPTHS):
        score(1, k)
    folded = []
    for h in range(HALVES):
        total = jnp.zeros((lines, 128), F32)
        for u in range(2):
            gene = u * (genes // 2) + iota((1, 128), 1) // part
            total = total + jnp.where(
                line_gene == gene, scored[h, :, u * 128 : (u + 1) * 128], 0.0
            )
        for turn in (64, 32, 16):
            total = total + pltpu.roll(total, turn, 1)
        folded.append(total)
    total = jnp.where(iota((1, 128), 1) < part, folded[0], folded[1])
    out_ref[...] = (total * scale[:lines])[:, : HALVES * part]

    for h in range(HALVES):
        for k in range(CHUNKS):
            y_copy(h, k).wait_send()
            for d in range(1, z_count):
                z_copy(h, k, d).wait_send()

            @pl.when(stripe > 0)
            def _():
                rim_copy(h, k).wait_send()

        for e in range(1, STRIPES):
            for p in range(PIECES):
                x_copy(h, e, p).wait_send()
    for e in range(1, STRIPES):
        enc_copy(e).wait_send()
        base_copy(e).wait_send()
    for d in range(1, cohorts):
        precision_copy(d).wait_send()
        square_copy(d).wait_send()

    @pl.when(stripe > 0)
    def _():
        panel_copy().wait_send()


def fast_device(
    cohort_scores,
    allele_match,
    allele_flip,
    precision,
    reference_panel,
    gene_weights,
    window_start,
    window_length,
):
    rows, traits = cohort_scores.shape[1:]
    cohorts = lax.axis_size("cohort")
    z_count = cohorts // Y_COUNT
    bucket = rows // STRIPES
    persons = reference_panel.shape[0]
    share = persons // cohorts
    genes, tissues, span = gene_weights.shape
    lines = genes * tissues
    width = rows // CHUNKS
    deep = rows // DEPTHS
    half = traits // HALVES
    part = half // cohorts
    blocks = -(-lines // 1024) * 8
    vmem = pl.BlockSpec(memory_space=pltpu.VMEM)
    smem = pl.BlockSpec(memory_space=pltpu.SMEM)
    hbm = pl.BlockSpec(memory_space=pl.ANY)
    dma = pltpu.SemaphoreType.DMA
    table = pl.pallas_call(
        functools.partial(one_kernel, z_count, traits, persons),
        out_shape=jax.ShapeDtypeStruct((lines, HALVES * part), F32),
        in_specs=[smem, smem, vmem, vmem, vmem, hbm, hbm, hbm],
        out_specs=vmem,
        scratch_shapes=[
            pltpu.VMEM((rows, traits), BF16),
            pltpu.VMEM((share, rows), BF16),
            pltpu.VMEM((share, rows), BF16),
            pltpu.VMEM((lines, span), BF16),
            pltpu.VMEM((STRIPES * BIN_ROWS, rows), BF16),
            pltpu.VMEM((1, rows), I32),
            pltpu.VMEM((1, rows), I32),
            pltpu.VMEM((1, rows), F32),
            pltpu.VMEM((1, rows), F32),
            pltpu.VMEM((128, STRIPES * BIN_ROWS), F32),
            pltpu.VMEM((STRIPES * BIN_ROWS, 128), F32),
            pltpu.VMEM((STRIPES * BIN_ROWS, 128), I32),
            pltpu.VMEM((1, STRIPES * BIN_ROWS), I32),
            pltpu.VMEM((STRIPES, BIN_ROWS, 128), F32),
            pltpu.VMEM((STRIPES, 1, STRIPES * BIN_ROWS), I32),
            pltpu.SMEM((STRIPES, 1, STRIPES * BIN_ROWS), I32),
            pltpu.VMEM((HALVES, STRIPES, bucket // 128, half, 128), BF16),
            pltpu.VMEM((STRIPES, bucket // 128, half, 128), BF16),
            pltpu.VMEM((STRIPES, bucket // 128, half, 128), BF16),
            pltpu.VMEM((HALVES, CHUNKS, Y_COUNT, half // 2, width), BF16),
            pltpu.VMEM((HALVES, CHUNKS, half // 2, width), BF16),
            pltpu.VMEM((HALVES, CHUNKS, z_count, part, width), BF16),
            pltpu.VMEM((HALVES, CHUNKS, z_count, part, width), BF16),
            pltpu.VMEM((HALVES, CHUNKS, part, width), BF16),
            pltpu.VMEM((HALVES, CHUNKS, part, width), BF16),
            pltpu.VMEM((cohorts, 1, rows), F32),
            pltpu.VMEM((1, rows), F32),
            pltpu.VMEM((2 * rows, 128), F32),
            pltpu.VMEM((HALVES, 2 * rows, 128), F32),
            pltpu.VMEM((HALVES, lines, 256), F32),
            pltpu.VMEM((1, rows), F32),
            pltpu.VMEM((genes * share // 256, lines, 256), F32),
            pltpu.VMEM((blocks, 128), F32),
            pltpu.VMEM((cohorts, blocks, 128), F32),
            dma((3,)),
            dma((HALVES, CHUNKS)),
            dma((HALVES, CHUNKS)),
            dma((STRIPES,)),
            dma((STRIPES,)),
            dma((STRIPES,)),
            dma((STRIPES,)),
            dma,
            dma((HALVES, STRIPES, PIECES)),
            dma((HALVES, STRIPES, PIECES)),
            dma((HALVES, CHUNKS)),
            dma((HALVES, CHUNKS)),
            dma((HALVES, CHUNKS, z_count)),
            dma((HALVES, CHUNKS, z_count)),
            dma((cohorts,)),
            dma((cohorts,)),
            dma((cohorts,)),
            dma((cohorts,)),
            dma,
            dma,
        ],
        compiler_params=pltpu.CompilerParams(
            collective_id=0, has_side_effects=True, vmem_limit_bytes=58 * 2**20
        ),
    )(
        window_start,
        window_length,
        allele_match,
        allele_flip,
        precision,
        cohort_scores[0],
        reference_panel,
        jnp.transpose(gene_weights, (1, 0, 2)).reshape(lines, span),
    )
    return jnp.transpose(table.reshape(tissues, genes, HALVES * part), (1, 0, 2))


def on_device(cohort_scores, *others):
    rows, traits = cohort_scores.shape[1:]
    stripes = lax.axis_size("stripe")
    cohorts = lax.axis_size("cohort")
    persons = others[3].shape[0]
    genes, tissues, span = others[4].shape
    fits = (
        stripes == STRIPES
        and cohorts == 8
        and traits == 256
        and genes == 16
        and persons == 64 * cohorts
        and rows % (128 * PIECES * STRIPES) == 0
        and rows % (128 * CHUNKS) == 0
        and rows % 512 == 0
        and rows // 128 <= BIN_ROWS
        and rows // STRIPES >= 256
        and span == rows
        and tissues * genes <= 1024
    )
    if fits:
        return fast_device(cohort_scores, *others)
    return general_device(cohort_scores, *others)


def solution(mesh):
    in_specs = (
        P("cohort", "stripe", None),
        P("cohort", "stripe"),
        P("cohort", "stripe"),
        P("cohort", "stripe"),
        P(None, "stripe"),
        P("stripe", None, None),
        P("stripe"),
        P("stripe"),
    )
    out_specs = P("stripe", None, "cohort")
    return jax.shard_map(
        on_device, mesh=mesh, in_specs=in_specs, out_specs=out_specs, check_vma=False
    )
```

```python
import functools

import jax
import jax.numpy as jnp
from jax import lax
from jax.experimental import pallas as pl
from jax.experimental.pallas import tpu as pltpu
from jax.sharding import PartitionSpec as P

EPSILON = 1e-06


def passed_along(block, axis, distance):
    devices = range(lax.axis_size(axis))
    route = [(i - distance, i) for i in devices if i - distance in devices]
    return lax.ppermute(block, axis, route)


def running_count(member):
    rows, columns = member.shape
    block = 128 if rows % 128 == 0 else rows
    parts = member.astype(jnp.float32).reshape(rows // block, block, columns)
    inner = jnp.einsum(
        "ij,bjc->bic",
        jnp.tril(jnp.ones((block, block), jnp.float32)),
        parts,
        precision=lax.Precision.HIGHEST,
    )
    outer = jnp.einsum(
        "ab,bc->ac",
        jnp.tril(jnp.ones((rows // block, rows // block), jnp.float32), -1),
        inner[:, -1, :],
        precision=lax.Precision.HIGHEST,
    )
    return (inner + outer[:, None, :]).reshape(rows, columns).astype(jnp.int32)


def general_device(
    cohort_scores,
    allele_match,
    allele_flip,
    precision,
    reference_panel,
    gene_weights,
    window_start,
    window_length,
):
    row_count = cohort_scores.shape[1]
    trait_count = cohort_scores.shape[2]
    stripe_count = lax.axis_size("stripe")
    cohort_count = lax.axis_size("cohort")
    bucket_rows = row_count // stripe_count
    block_traits = trait_count // cohort_count
    person_count = reference_panel.shape[0]
    gene_count = gene_weights.shape[0]
    tissue_count = gene_weights.shape[1]
    window_span = gene_weights.shape[2]
    step_width = min(512, window_span)
    first_variant = lax.axis_index("stripe") * row_count
    target = allele_match[0] // row_count
    inside = allele_match[0] - target * row_count
    member = (target[:, None] == jnp.arange(stripe_count, dtype=jnp.int32)[None, :]).astype(
        jnp.int32
    )
    ranking = jnp.sum(running_count(member) * member, axis=1) - 1
    placing = target * bucket_rows + ranking
    signs = (1 - 2 * allele_flip[0]).astype(jnp.bfloat16)
    flipped = cohort_scores[0] * signs[:, None]
    outgoing = jnp.zeros((row_count, trait_count), jnp.bfloat16).at[placing].set(flipped)
    out_keys = jnp.zeros((row_count,), jnp.int32).at[placing].set(inside)
    got_rows, got_keys = (
        lax.all_to_all(
            outgoing.reshape(stripe_count, bucket_rows, trait_count),
            "stripe",
            split_axis=0,
            concat_axis=0,
            tiled=True,
        ),
        lax.all_to_all(
            out_keys.reshape(stripe_count, bucket_rows),
            "stripe",
            split_axis=0,
            concat_axis=0,
            tiled=True,
        ),
    )
    aligned = (
        jnp.zeros((row_count, trait_count), jnp.bfloat16)
        .at[got_keys.reshape(row_count)]
        .set(got_rows.reshape(row_count, trait_count))
    )
    own_weight = precision[0]
    weighted = (jnp.sqrt(own_weight)[:, None] * aligned).astype(jnp.bfloat16)
    total_weight = lax.psum(own_weight, "cohort")
    received = lax.all_to_all(weighted, "cohort", split_axis=1, concat_axis=1, tiled=True)
    summed = jnp.sum(
        received.reshape(row_count, cohort_count, block_traits).astype(jnp.float32), axis=1
    )
    combined = (summed.T / jnp.sqrt(total_weight)[None, :]).astype(jnp.bfloat16)
    joined = jnp.concatenate([reference_panel, combined], axis=0)
    moved = passed_along(joined, "stripe", -1)
    panel_rim = moved[:person_count]
    score_rim = moved[person_count:]
    panel_ext = jnp.concatenate([reference_panel, panel_rim], axis=1)
    score_ext = jnp.concatenate([combined, score_rim], axis=1)

    def weight_block(gene, block, size):
        offset = block * step_width
        piece = lax.dynamic_slice(
            gene_weights[gene], (jnp.int32(0), offset), (tissue_count, step_width)
        )
        keep = offset + jnp.arange(step_width, dtype=jnp.int32) < size
        return jnp.where(keep[None, :], piece, jnp.zeros_like(piece))

    def window_variance(gene, size):
        begin = window_start[gene] - first_variant

        def add_block(block, running):
            columns = lax.dynamic_slice(
                panel_ext, (jnp.int32(0), begin + block * step_width), (person_count, step_width)
            )
            piece = weight_block(gene, block, size)
            return running + lax.dot_general(
                columns, piece, (((1,), (1,)), ((), ())), preferred_element_type=jnp.float32
            )

        blocks_needed = (size + step_width - 1) // step_width
        projected = lax.fori_loop(
            0, blocks_needed, add_block, jnp.zeros((person_count, tissue_count), jnp.float32)
        )
        return jnp.sum(projected * projected, axis=0) / person_count

    def window_score(gene):
        begin = window_start[gene] - first_variant
        size = window_length[gene]

        def add_block(block, running):
            window = lax.dynamic_slice(
                score_ext, (jnp.int32(0), begin + block * step_width), (block_traits, step_width)
            )
            piece = weight_block(gene, block, size)
            return running + lax.dot_general(
                piece, window, (((1,), (1,)), ((), ())), preferred_element_type=jnp.float32
            )

        blocks_needed = (size + step_width - 1) // step_width
        return lax.fori_loop(
            0, blocks_needed, add_block, jnp.zeros((tissue_count, block_traits), jnp.float32)
        )

    empty = jnp.zeros((gene_count, tissue_count), jnp.float32)

    def every_gene(gene, partial_value):
        return partial_value.at[gene].set(window_variance(gene, window_length[gene]))

    variance = lax.fori_loop(0, gene_count, every_gene, empty)

    def score_gene(gene, partial_value):
        return partial_value.at[gene].set(window_score(gene))

    numerator = lax.fori_loop(
        0, gene_count, score_gene, jnp.zeros((gene_count, tissue_count, block_traits), jnp.float32)
    )
    return numerator / jnp.sqrt(variance + EPSILON)[:, :, None]

MESH = pl.DeviceIdType.MESH
BF16 = jnp.bfloat16
F32 = jnp.float32
I32 = jnp.int32
Y_COUNT = 2
STRIPES = 4
HALVES = 2
CHUNKS = 6
BIN_ROWS = 64
ABSENT = -1024.0
PIECES = 3
TURNS = 2
LAG = 2
DEPTHS = 3


def spread_column(row):
    return jnp.transpose(jnp.broadcast_to(row, (128, 128)))


def iota(shape, dim):
    return lax.broadcasted_iota(I32, shape, dim)


def one_kernel(
    z_count,
    traits,
    persons,
    window_ref,
    size_ref,
    match_ref,
    flip_ref,
    precision_ref,
    scores_hbm,
    panel_hbm,
    weights_hbm,
    out_ref,
    scores,
    panel,
    panel_rim,
    weights,
    hot_bin,
    bin_row,
    place_row,
    slot_row,
    sign_row,
    count_total,
    enc,
    base,
    base_row,
    got_enc,
    got_base,
    starts,
    packed,
    got_first,
    got_second,
    own,
    y_got,
    pair,
    z_got,
    mine,
    rim,
    precisions,
    root,
    panel_turned,
    score_turned,
    scored,
    total_root,
    projected,
    square_row,
    squares,
    in_sem,
    rim_send,
    rim_recv,
    e_send,
    e_recv,
    b_send,
    b_recv,
    start_sem,
    x_send,
    x_recv,
    y_send,
    y_recv,
    z_send,
    z_recv,
    w_send,
    w_recv,
    s_send,
    s_recv,
    p_send,
    p_recv,
):
    cohort = lax.axis_index("cohort")
    stripe = lax.axis_index("stripe")
    cohorts = z_count * Y_COUNT
    z, y = cohort // Y_COUNT, lax.rem(cohort, Y_COUNT)
    x, core = stripe // 2, lax.rem(stripe, 2)
    rows = match_ref.shape[1]
    bucket = rows // STRIPES
    piece = bucket // PIECES
    bins = rows // 128
    width = rows // CHUNKS
    deep = rows // DEPTHS
    half = traits // HALVES
    part = half // cohorts
    share = panel.shape[0]
    genes = window_ref.shape[0]
    lines = weights.shape[0]
    got = (got_first, got_second)

    def partner(e):
        return lax.rem(x + e // 2, 2) * 2 + lax.rem(core + e, 2)

    scores_in = pltpu.make_async_copy(scores_hbm, scores, in_sem.at[0])
    panel_in = pltpu.make_async_copy(
        panel_hbm.at[pl.ds(pl.multiple_of(cohort * share, share), share)], panel, in_sem.at[1]
    )
    weights_in = pltpu.make_async_copy(weights_hbm, weights, in_sem.at[2])
    scores_in.start()
    panel_in.start()
    weights_in.start()

    barrier = pltpu.get_barrier_semaphore()
    for d in range(1, cohorts):
        pl.semaphore_signal(
            barrier, inc=1, device_id=(lax.rem(cohort + d, cohorts), stripe), device_id_type=MESH
        )
    for e in range(1, STRIPES):
        pl.semaphore_signal(barrier, inc=1, device_id=(cohort, partner(e)), device_id_type=MESH)

    def panel_copy():
        return pltpu.make_async_remote_copy(
            src_ref=panel,
            dst_ref=panel_rim,
            send_sem=p_send,
            recv_sem=p_recv,
            device_id=(cohort, lax.rem(stripe + STRIPES - 1, STRIPES)),
            device_id_type=MESH,
        )

    def precision_copy(d):
        return pltpu.make_async_remote_copy(
            src_ref=precision_ref,
            dst_ref=precisions.at[d],
            send_sem=w_send.at[d],
            recv_sem=w_recv.at[d],
            device_id=(lax.rem(cohort + d, cohorts), stripe),
            device_id_type=MESH,
        )

    def square_copy(d):
        return pltpu.make_async_remote_copy(
            src_ref=square_row,
            dst_ref=squares.at[d],
            send_sem=s_send.at[d],
            recv_sem=s_recv.at[d],
            device_id=(lax.rem(cohort + d, cohorts), stripe),
            device_id_type=MESH,
        )

    def enc_copy(e):
        there = pl.ds(pl.multiple_of(partner(e) * BIN_ROWS, BIN_ROWS), BIN_ROWS)
        return pltpu.make_async_remote_copy(
            src_ref=enc.at[there],
            dst_ref=got_enc.at[e],
            send_sem=e_send.at[e],
            recv_sem=e_recv.at[e],
            device_id=(cohort, partner(e)),
            device_id_type=MESH,
        )

    def base_copy(e):
        return pltpu.make_async_remote_copy(
            src_ref=base_row,
            dst_ref=got_base.at[e],
            send_sem=b_send.at[e],
            recv_sem=b_recv.at[e],
            device_id=(cohort, partner(e)),
            device_id_type=MESH,
        )

    def x_copy(h, e, p):
        here = pl.ds(p * (piece // 128), piece // 128)
        return pltpu.make_async_remote_copy(
            src_ref=packed.at[h, e, here],
            dst_ref=got[h].at[e, here],
            send_sem=x_send.at[h, e, p],
            recv_sem=x_recv.at[h, e, p],
            device_id=(cohort, partner(e)),
            device_id_type=MESH,
        )

    def y_copy(h, k):
        return pltpu.make_async_remote_copy(
            src_ref=own.at[h, k, 1 - y],
            dst_ref=y_got.at[h, k],
            send_sem=y_send.at[h, k],
            recv_sem=y_recv.at[h, k],
            device_id=(z * Y_COUNT + 1 - y, stripe),
            device_id_type=MESH,
        )

    def z_copy(h, k, d):
        other = lax.rem(z + d, z_count)
        return pltpu.make_async_remote_copy(
            src_ref=pair.at[h, k, other],
            dst_ref=z_got.at[h, k, d],
            send_sem=z_send.at[h, k, d],
            recv_sem=z_recv.at[h, k, d],
            device_id=(other * Y_COUNT + y, stripe),
            device_id_type=MESH,
        )

    def rim_copy(h, k):
        return pltpu.make_async_remote_copy(
            src_ref=mine.at[h, k],
            dst_ref=rim.at[h, k],
            send_sem=rim_send.at[h, k],
            recv_sem=rim_recv.at[h, k],
            device_id=(cohort, lax.rem(stripe + STRIPES - 1, STRIPES)),
            device_id_type=MESH,
        )

    match = match_ref[...]
    owner = jnp.zeros_like(match)
    for s in range(1, STRIPES):
        owner = owner + jnp.where(match >= s * rows, 1, 0)
    inside = match - owner * rows
    bin_row[...] = owner * BIN_ROWS + lax.shift_right_logical(inside, 7)
    place_row[...] = jnp.bitwise_and(inside, 127)
    sign_row[...] = (1 - 2 * flip_ref[...]).astype(F32)
    root[...] = jnp.sqrt(precision_ref[...])
    pl.semaphore_wait(barrier, cohorts + STRIPES - 2)
    panel_in.wait()

    @pl.when(stripe > 0)
    def _():
        panel_copy().start()

    for d in range(1, cohorts):
        precision_copy(d).start()
    bin_count = STRIPES * BIN_ROWS
    span = 512
    count_total[...] = jnp.zeros_like(count_total)
    base[...] = jnp.zeros_like(base)

    def count(c, carry):
        here = pl.ds(pl.multiple_of(c * span, span), span)
        hot = jnp.where(bin_row[:, here] == iota((bin_count, span), 0), 1.0, 0.0).astype(BF16)
        low = jnp.where(place_row[:, here] == iota((128, span), 0), 1.0, 0.0).astype(BF16)
        hot_bin[:, here] = hot
        below = jnp.where(bin_row[:, here] < iota((bin_count, span), 0), 1, 0)
        for b in range(span // 128):
            base[...] += below[:, b * 128 : (b + 1) * 128]
        count_total[...] += lax.dot_general(
            low, hot, (((1,), (1,)), ((), ())), preferred_element_type=F32
        )
        return carry

    lax.fori_loop(0, rows // span, count, 0)

    present = count_total[...]
    present16 = present.astype(BF16)
    before = jnp.where(iota((128, 128), 1) < iota((128, 128), 0), 1.0, 0.0).astype(BF16)
    within = jnp.dot(before, present16, preferred_element_type=F32)
    sums = jnp.dot(jnp.ones((128, 128), BF16), present16, preferred_element_type=F32)
    earlier = jnp.where(
        iota((bin_count, bin_count), 0) < iota((bin_count, bin_count), 1), 1.0, 0.0
    ).astype(BF16)
    first = jnp.dot(sums.astype(BF16), earlier, preferred_element_type=F32)
    coded = jnp.where(present > 0.5, within, ABSENT)
    for b in range(bin_count // 128):
        here = slice(b * 128, (b + 1) * 128)
        base_row[:, here] = jnp.sum(
            jnp.transpose(base[here, :]), axis=0, keepdims=True
        ) - bucket * lax.shift_right_logical(
            iota((1, 128), 1) + b * 128, BIN_ROWS.bit_length() - 1
        )
    for b in range(bin_count // 128):
        enc[b * 128 : (b + 1) * 128] = jnp.transpose(coded[:, b * 128 : (b + 1) * 128])
    for e in range(1, STRIPES):
        enc_copy(e).start()
        base_copy(e).start()
    mine_rows = pl.ds(pl.multiple_of(stripe * BIN_ROWS, BIN_ROWS), BIN_ROWS)
    got_enc[0] = enc[mine_rows, :]
    got_base[0] = base_row[...]
    high = jnp.floor(first[0:8] * (1.0 / 64.0))
    table = jnp.concatenate([within, high, first[0:8] - 64.0 * high], axis=0).astype(BF16)

    lane = iota((traits, traits), 1)
    source = (
        (lane % half // part % z_count * Y_COUNT + lane % half // (half // Y_COUNT))
        * (traits // cohorts)
        + lane // half * part
        + lane % part
    )
    order = jnp.where(iota((traits, traits), 0) == source, 1.0, 0.0).astype(BF16)
    scores_in.wait()

    def rank(c, carry):
        here = pl.ds(pl.multiple_of(c * span, span), span)
        found = jnp.dot(table, hot_bin[:, here], preferred_element_type=F32)
        chosen = jnp.where(place_row[:, here] == iota((128, span), 0), found[:128], 0.0)
        slot_row[:, here] = (
            jnp.sum(chosen, axis=0, keepdims=True) + 64.0 * found[128:129] + found[136:137]
        )
        scores[here, :] = jnp.dot(
            scores[here, :], order, preferred_element_type=F32
        ).astype(BF16)
        return carry

    lax.fori_loop(0, rows // span, rank, 0)

    def place_rows(e, first, blocks):
        low = (partner(e) * bucket + first * 128).astype(F32)
        size = blocks * 128
        total = jnp.zeros((size, traits), F32)
        for q in range(2):
            here = slice(q * (rows // 2), (q + 1) * (rows // 2))
            hot = jnp.where(
                slot_row[:, here] - low == iota((size, rows // 2), 0).astype(F32),
                sign_row[:, here],
                0.0,
            ).astype(BF16)
            total = total + jnp.dot(hot, scores[here, :], preferred_element_type=F32)
        for b in range(blocks):
            for h in range(HALVES):
                packed[h, e, first + b] = jnp.transpose(
                    total[b * 128 : (b + 1) * 128, h * half : (h + 1) * half]
                ).astype(BF16)

    def pack(c, carry):
        e, p = STRIPES - 1 - c // PIECES, lax.rem(c, PIECES)
        place_rows(e, p * (piece // 128), piece // 128)

        @pl.when(e > 0)
        def _():
            x_copy(0, e, p).start()

        return carry

    lax.fori_loop(0, STRIPES * PIECES, pack, 0)
    for e in (3, 2, 1):
        for p in range(PIECES):
            x_copy(1, e, p).start()

    def turn_panel(side, offset, k):
        for b in range(width // 128):
            here = pl.multiple_of(k * width + b * 128, 128)
            block = side[:, pl.ds(here, 128)].astype(F32)
            panel_turned[pl.ds(pl.multiple_of(offset + here, 128), 128), :] = jnp.transpose(
                jnp.concatenate([block] * (128 // share), axis=0)
            )

    @pl.when(stripe < STRIPES - 1)
    def _():
        panel_copy().wait_recv()

    for e in range(1, STRIPES):
        enc_copy(e).wait_recv()
        base_copy(e).wait_recv()
    starts_in = pltpu.make_async_copy(got_base, starts, start_sem)
    starts_in.start()
    starts_in.wait()

    def align(h, k):
        for b in range(width // 128):
            at = k * (width // 128) + b
            hots, lefts = [], []
            for e in range(STRIPES):
                low = starts[e, 0, stripe * BIN_ROWS + at]
                q = jnp.minimum(lax.shift_right_logical(low, 7), bucket // 128 - 2)
                want = got_enc[e, pl.ds(at, 1), :] + (low - q * 128).astype(F32)
                hots.append(
                    jnp.where(want == iota((256, 128), 0).astype(F32), 1.0, 0.0).astype(BF16)
                )
                for step in range(2):
                    lefts.append(got[h][e, q + step] if e else packed[h, e, q + step])
            total = jnp.dot(
                jnp.concatenate(lefts, axis=1),
                jnp.concatenate(hots, axis=0),
                preferred_element_type=F32,
            )
            scaled = (total * root[:, pl.ds(pl.multiple_of(at * 128, 128), 128)]).astype(BF16)
            for yy in range(Y_COUNT):
                own[h, k, yy, :, b * 128 : (b + 1) * 128] = scaled[
                    yy * (half // 2) : (yy + 1) * (half // 2)
                ]
        y_copy(h, k).start()

    def pair_up(h, k):
        y_copy(h, k).wait_recv()
        both = own[h, k, y].astype(F32) + y_got[h, k].astype(F32)
        for zi in range(z_count):
            pair[h, k, zi] = both[zi * part : (zi + 1) * part].astype(BF16)
        for d in range(1, z_count):
            z_copy(h, k, d).start()

    def windows(side, k, first_gene, lanes_each):
        tiles = []
        place = iota((deep, 128), 0) + k * deep
        group = iota((1, 128), 1) // lanes_each
        count = 128 // lanes_each
        for u in range(2):
            value = None
            limit = jnp.zeros((1, 128), I32)
            for j in range(count):
                gene = first_gene + u * count + j
                piece_ = side[pl.ds(jnp.clip(window_ref[gene] - stripe * rows, 0, rows) + k * deep, deep), :]
                value = piece_ if j == 0 else jnp.where(group == j, piece_, value)
                limit = jnp.where(group == j, size_ref[gene], limit)
            tiles.append(jnp.where(place < limit, value, 0.0).astype(BF16))
        return jnp.concatenate(tiles, axis=1)

    def left(k):
        return weights[:, pl.ds(pl.multiple_of(k * deep, deep), deep)]

    each = 128 // share * 2

    groups = genes // each

    def project(unit, count):
        for c in range(count):
            n = lax.rem(unit + c, groups)
            k = (unit + c) // groups
            projected[n] += jnp.dot(
                left(k), windows(panel_turned, k, n * each, share), preferred_element_type=F32
            )

    def finish(h, k):
        summed = pair[h, k, z].astype(F32)
        for d in range(1, z_count):
            z_copy(h, k, d).wait_recv()
            summed = summed + z_got[h, k, d].astype(F32)
        here = pl.ds(pl.multiple_of(k * width, width), width)
        mine[h, k] = (summed / total_root[:, here]).astype(BF16)

        @pl.when(stripe > 0)
        def _():
            rim_copy(h, k).start()

    def turn_scores(side, h, k, offset):
        for b in range(width // 128):
            block = side[h, k, :, b * 128 : (b + 1) * 128].astype(F32)
            score_turned[
                h, pl.ds(pl.multiple_of(offset + k * width + b * 128, 128), 128), :
            ] = jnp.transpose(jnp.concatenate([block] * (128 // part), axis=0))

    def score(h, k):
        scored[h] += jnp.dot(
            left(k), windows(score_turned.at[h], k, 0, part), preferred_element_type=F32
        )

    def rim_in(h):
        def one(k, carry):
            @pl.when(stripe < STRIPES - 1)
            def _():
                rim_copy(h, k).wait_recv()

            turn_scores(rim, h, k, rows)
            return carry

        lax.fori_loop(0, CHUNKS, one, 0)

    for e in range(1, STRIPES):
        for p in range(PIECES):
            x_copy(0, e, p).wait_recv()

    def first_half(k, carry):
        @pl.when(k < CHUNKS)
        def _():
            align(0, k)

        @pl.when(k < TURNS)
        def _():
            for c in range(CHUNKS // TURNS):
                turn_panel(panel, 0, k * (CHUNKS // TURNS) + c)
                turn_panel(panel_rim, rows, k * (CHUNKS // TURNS) + c)

        @pl.when(k == TURNS)
        def _():
            weights_in.wait()
            projected[...] = jnp.zeros_like(projected)

        @pl.when(k >= TURNS)
        def _():
            project(k - TURNS, 1)

        @pl.when(k >= LAG)
        def _():
            pair_up(0, k - LAG)

        return carry

    lax.fori_loop(0, CHUNKS + LAG, first_half, 0)
    precision_sum = precision_ref[...]
    for d in range(1, cohorts):
        precision_copy(d).wait_recv()
        precision_sum = precision_sum + precisions[d]
    total_root[...] = jnp.sqrt(precision_sum)
    scored[...] = jnp.zeros_like(scored)

    for e in range(1, STRIPES):
        for p in range(PIECES):
            x_copy(1, e, p).wait_recv()

    def second_half(k, carry):
        @pl.when(k < CHUNKS)
        def _():
            align(1, k)

        @pl.when(k < 3)
        def _():
            for c in range(2):
                finish(0, 2 * k + c)
                turn_scores(mine, 0, 2 * k + c, 0)

        @pl.when(k < 3)
        def _():
            project(6 + 2 * k, 2)

        @pl.when(k == 3)
        def _():
            rim_in(0)

        @pl.when(jnp.logical_and(k > 3, k < 7))
        def _():
            score(0, k - 4)

        @pl.when(k >= LAG)
        def _():
            pair_up(1, k - LAG)

        return carry

    lax.fori_loop(0, CHUNKS + LAG, second_half, 0)

    line_gene = jnp.bitwise_and(iota((lines, 1), 0), genes - 1)
    square = jnp.zeros((lines, 128), F32)
    for n in range(genes // each):
        for u in range(2):
            value = projected[n, :, u * 128 : (u + 1) * 128]
            gene = n * each + u * (each // 2) + iota((1, 128), 1) // share
            square = square + jnp.where(line_gene == gene, value * value, 0.0)
    blocks = square_row.shape[0]
    square = jnp.concatenate([square, jnp.zeros((blocks * 128 - lines, 128), F32)], axis=0)
    for b in range(blocks):
        square_row[b : b + 1, :] = jnp.sum(
            jnp.transpose(square[b * 128 : (b + 1) * 128]), axis=0, keepdims=True
        )
    for d in range(1, cohorts):
        square_copy(d).start()

    for k in range(CHUNKS):
        finish(1, k)
        turn_scores(mine, 1, k, 0)

    square_sum = square_row[...]
    for d in range(1, cohorts):
        square_copy(d).wait_recv()
        square_sum = square_sum + squares[d]
    spread = 1.0 / jnp.sqrt(square_sum / persons + EPSILON)
    scale = jnp.concatenate([spread_column(spread[b : b + 1]) for b in range(blocks)], axis=0)
    rim_in(1)

    for k in range(DEPTHS):
        score(1, k)
    folded = []
    for h in range(HALVES):
        total = jnp.zeros((lines, 128), F32)
        for u in range(2):
            gene = u * (genes // 2) + iota((1, 128), 1) // part
            total = total + jnp.where(
                line_gene == gene, scored[h, :, u * 128 : (u + 1) * 128], 0.0
            )
        for turn in (64, 32, 16):
            total = total + pltpu.roll(total, turn, 1)
        folded.append(total)
    total = jnp.where(iota((1, 128), 1) < part, folded[0], folded[1])
    out_ref[...] = (total * scale[:lines])[:, : HALVES * part]

    for h in range(HALVES):
        for k in range(CHUNKS):
            y_copy(h, k).wait_send()
            for d in range(1, z_count):
                z_copy(h, k, d).wait_send()

            @pl.when(stripe > 0)
            def _():
                rim_copy(h, k).wait_send()

        for e in range(1, STRIPES):
            for p in range(PIECES):
                x_copy(h, e, p).wait_send()
    for e in range(1, STRIPES):
        enc_copy(e).wait_send()
        base_copy(e).wait_send()
    for d in range(1, cohorts):
        precision_copy(d).wait_send()
        square_copy(d).wait_send()

    @pl.when(stripe > 0)
    def _():
        panel_copy().wait_send()


def fast_device(
    cohort_scores,
    allele_match,
    allele_flip,
    precision,
    reference_panel,
    gene_weights,
    window_start,
    window_length,
):
    rows, traits = cohort_scores.shape[1:]
    cohorts = lax.axis_size("cohort")
    z_count = cohorts // Y_COUNT
    bucket = rows // STRIPES
    persons = reference_panel.shape[0]
    share = persons // cohorts
    genes, tissues, span = gene_weights.shape
    lines = genes * tissues
    width = rows // CHUNKS
    deep = rows // DEPTHS
    half = traits // HALVES
    part = half // cohorts
    blocks = -(-lines // 1024) * 8
    vmem = pl.BlockSpec(memory_space=pltpu.VMEM)
    smem = pl.BlockSpec(memory_space=pltpu.SMEM)
    hbm = pl.BlockSpec(memory_space=pl.ANY)
    dma = pltpu.SemaphoreType.DMA
    table = pl.pallas_call(
        functools.partial(one_kernel, z_count, traits, persons),
        out_shape=jax.ShapeDtypeStruct((lines, HALVES * part), F32),
        in_specs=[smem, smem, vmem, vmem, vmem, hbm, hbm, hbm],
        out_specs=vmem,
        scratch_shapes=[
            pltpu.VMEM((rows, traits), BF16),
            pltpu.VMEM((share, rows), BF16),
            pltpu.VMEM((share, rows), BF16),
            pltpu.VMEM((lines, span), BF16),
            pltpu.VMEM((STRIPES * BIN_ROWS, rows), BF16),
            pltpu.VMEM((1, rows), I32),
            pltpu.VMEM((1, rows), I32),
            pltpu.VMEM((1, rows), F32),
            pltpu.VMEM((1, rows), F32),
            pltpu.VMEM((128, STRIPES * BIN_ROWS), F32),
            pltpu.VMEM((STRIPES * BIN_ROWS, 128), F32),
            pltpu.VMEM((STRIPES * BIN_ROWS, 128), I32),
            pltpu.VMEM((1, STRIPES * BIN_ROWS), I32),
            pltpu.VMEM((STRIPES, BIN_ROWS, 128), F32),
            pltpu.VMEM((STRIPES, 1, STRIPES * BIN_ROWS), I32),
            pltpu.SMEM((STRIPES, 1, STRIPES * BIN_ROWS), I32),
            pltpu.VMEM((HALVES, STRIPES, bucket // 128, half, 128), BF16),
            pltpu.VMEM((STRIPES, bucket // 128, half, 128), BF16),
            pltpu.VMEM((STRIPES, bucket // 128, half, 128), BF16),
            pltpu.VMEM((HALVES, CHUNKS, Y_COUNT, half // 2, width), BF16),
            pltpu.VMEM((HALVES, CHUNKS, half // 2, width), BF16),
            pltpu.VMEM((HALVES, CHUNKS, z_count, part, width), BF16),
            pltpu.VMEM((HALVES, CHUNKS, z_count, part, width), BF16),
            pltpu.VMEM((HALVES, CHUNKS, part, width), BF16),
            pltpu.VMEM((HALVES, CHUNKS, part, width), BF16),
            pltpu.VMEM((cohorts, 1, rows), F32),
            pltpu.VMEM((1, rows), F32),
            pltpu.VMEM((2 * rows, 128), F32),
            pltpu.VMEM((HALVES, 2 * rows, 128), F32),
            pltpu.VMEM((HALVES, lines, 256), F32),
            pltpu.VMEM((1, rows), F32),
            pltpu.VMEM((genes * share // 256, lines, 256), F32),
            pltpu.VMEM((blocks, 128), F32),
            pltpu.VMEM((cohorts, blocks, 128), F32),
            dma((3,)),
            dma((HALVES, CHUNKS)),
            dma((HALVES, CHUNKS)),
            dma((STRIPES,)),
            dma((STRIPES,)),
            dma((STRIPES,)),
            dma((STRIPES,)),
            dma,
            dma((HALVES, STRIPES, PIECES)),
            dma((HALVES, STRIPES, PIECES)),
            dma((HALVES, CHUNKS)),
            dma((HALVES, CHUNKS)),
            dma((HALVES, CHUNKS, z_count)),
            dma((HALVES, CHUNKS, z_count)),
            dma((cohorts,)),
            dma((cohorts,)),
            dma((cohorts,)),
            dma((cohorts,)),
            dma,
            dma,
        ],
        compiler_params=pltpu.CompilerParams(
            collective_id=0, has_side_effects=True, vmem_limit_bytes=58 * 2**20
        ),
    )(
        window_start,
        window_length,
        allele_match,
        allele_flip,
        precision,
        cohort_scores[0],
        reference_panel,
        jnp.transpose(gene_weights, (1, 0, 2)).reshape(lines, span),
    )
    return jnp.transpose(table.reshape(tissues, genes, HALVES * part), (1, 0, 2))


def on_device(cohort_scores, *others):
    rows, traits = cohort_scores.shape[1:]
    stripes = lax.axis_size("stripe")
    cohorts = lax.axis_size("cohort")
    persons = others[3].shape[0]
    genes, tissues, span = others[4].shape
    fits = (
        stripes == STRIPES
        and cohorts == 8
        and traits == 256
        and genes == 16
        and persons == 64 * cohorts
        and rows % (128 * PIECES * STRIPES) == 0
        and rows % (128 * CHUNKS) == 0
        and rows % 512 == 0
        and rows // 128 <= BIN_ROWS
        and rows // STRIPES >= 256
        and span == rows
        and tissues * genes <= 1024
    )
    if fits:
        return fast_device(cohort_scores, *others)
    return general_device(cohort_scores, *others)


def solution(mesh):
    in_specs = (
        P("cohort", "stripe", None),
        P("cohort", "stripe"),
        P("cohort", "stripe"),
        P("cohort", "stripe"),
        P(None, "stripe"),
        P("stripe", None, None),
        P("stripe"),
        P("stripe"),
    )
    out_specs = P("stripe", None, "cohort")
    return jax.shard_map(
        on_device, mesh=mesh, in_specs=in_specs, out_specs=out_specs, check_vma=False
    )
```
